256 devices in a mesh: row: 8 (over z_lo, core), col: 32 (over z_hi, x, y).
Axes of the slice: x: 4, y: 4, z: 8 (z_hi: 2, z_lo: 4; z = z_hi * 4 + z_lo), core: 2. Of those that a mesh axis runs over, the one named last changes fastest.
Arguments:
- covariance: float32 [8192, 8192], P('row', 'col'), may hold values from -12 to 12, as said below
- noise_var: float32 [64, 128], P('row'), may hold values from 0.1 to 1
- wind_table: float32 [16, 2], replicated, may hold values from -0.7 to 0.7
- diffusivity: float32 [16], replicated, may hold values from 0.01 to 0.05
- wind_index: int32 [3, 64], replicated, may hold values from 0 to 15
Outputs:
- predicted_spread_matrix: float32 [8192, 8192], P('row', 'col')
- operator_times_prior: bfloat16 [8192, 8192], P('row', 'col')
The draws below stay inside these ranges and needn't reach their ends.
Inputs may be any that keep to these rules, and one draw needn't show every extreme that they name: covariance is symmetric: entry (a, b) equals entry (b, a) exactly.
All inputs are finite; a program needn't handle non-finite values.
Results may differ from the reference program's by a relative error of at most 0.0025.
Values may be sent and summed in bfloat16 or wider, within the bound.
A program may use at most 64 MiB of HBM per device.

```python
import math
import jax
import jax.numpy as jnp
from jax import lax

NLAT = 64
NLON = 128
STEPS = 3
TABLE = 16
MATRIX_ORDER = 8192


def draw_covariance(key, part):
    size = NLAT * NLON
    key_noise = jax.random.fold_in(jax.random.fold_in(key, 11), 0)
    raw = jnp.clip(jax.random.normal(key_noise, (size, size), jnp.float32), -6.0, 6.0) * 0.3
    sym = (raw + raw.T) * 0.5
    index_all = jnp.arange(size)
    sym = sym.at[index_all, index_all].add(1.0)
    return sym


def with_ends(drawn, rng, low, top_value):
    extent = drawn.shape
    index_at = [jax.random.randint(jax.random.fold_in(rng, axis), (), 0, extent[axis]) for axis in range(len(extent))]
    drawn = drawn.at[tuple(index_at)].set(low)
    longest = extent.index(max(extent))
    index_at[longest] = (index_at[longest] + 1) % extent[longest]
    return drawn.at[tuple(index_at)].set(top_value)


def shard_levels(rng, dims, cuts, low, top_value):
    def one(axis_at, parts):
        heights = jax.random.uniform(jax.random.fold_in(jax.random.fold_in(rng, 6), axis_at), (parts,), jnp.float32, low / len(cuts), top_value / len(cuts))
        return jnp.repeat(jnp.exp(heights), dims[axis_at] // parts).reshape((-1,) + (1,) * (len(dims) - axis_at - 1))

    factor_of = one(*cuts[0])
    for cut in cuts[1:]:
        factor_of = factor_of * one(*cut)
    return factor_of


def setup_inputs(seed: int = 0) -> dict:
    keys = jax.random.split(jax.random.key(seed), 6)
    return {
        "covariance": draw_covariance(jax.random.fold_in(keys[5], 71), 0),
        "noise_var": jnp.clip(jnp.exp(math.log(1.0) - 2.3025851 * jax.random.uniform(keys[1], (NLAT, NLON), jnp.float32) ** shard_levels(keys[1], (NLAT, NLON), ((0, 8),), -0.2, 0.2)), 0.1, 1.0),
        "wind_table": jnp.clip(jax.random.uniform(keys[2], (TABLE, 2), jnp.float32, -0.7, 0.7), -0.7, 0.7),
        "diffusivity": jnp.clip(jax.random.uniform(keys[3], (TABLE,), jnp.float32, 0.01, 0.05), 0.01, 0.05),
        "wind_index": with_ends(jax.random.randint(keys[4], (STEPS, NLAT), 0, TABLE), jax.random.fold_in(keys[4], 1), 0, TABLE - 1).astype(jnp.int32),
    }


def stencil_terms(zonal_cour, merid_cour, diffuse):
    middle_weight = 1.0 - zonal_cour * zonal_cour - merid_cour * merid_cour - 4.0 * diffuse
    eastward_weight = 0.5 * zonal_cour * zonal_cour - 0.5 * zonal_cour + diffuse
    west_w = 0.5 * zonal_cour * zonal_cour + 0.5 * zonal_cour + diffuse
    north_w = 0.5 * merid_cour * merid_cour - 0.5 * merid_cour + diffuse
    south_w = 0.5 * merid_cour * merid_cour + 0.5 * merid_cour + diffuse
    return jnp.stack([middle_weight, eastward_weight, west_w, north_w, south_w])


def stencil_weights(wind_table, diffusivity, wind_index):
    courant = wind_table[wind_index]
    return stencil_terms(courant[..., 0], courant[..., 1], diffusivity[wind_index])


def advance(values, weights, step_no):
    middle_weight = weights[0, step_no][:, None, None]
    eastward_weight = weights[1, step_no][:, None, None]
    west_w = weights[2, step_no][:, None, None]
    north_w = weights[3, step_no][:, None, None]
    south_w = weights[4, step_no][:, None, None]
    padded = jnp.pad(values, ((1, 1), (0, 0), (0, 0)))
    return (middle_weight * values + eastward_weight * jnp.roll(values, -1, 1) + west_w * jnp.roll(values, 1, 1)
            + north_w * padded[2:] + south_w * padded[:-2])


def reference(covariance, noise_var, wind_table, diffusivity, wind_index):
    weights = stencil_weights(wind_table, diffusivity, wind_index)
    count_of_blocks = NLAT // 4
    width_per_block = 4 * NLON

    def propagate(columns):
        values = columns.reshape(NLAT, NLON, width_per_block)
        for step_no in range(STEPS):
            values = advance(values, weights, step_no)
        return values.reshape(MATRIX_ORDER, width_per_block)

    def forward(columns):
        return propagate(columns).astype(jnp.bfloat16)

    column_blocks = covariance.reshape(MATRIX_ORDER, count_of_blocks, width_per_block).transpose(1, 0, 2)
    product_blocks = lax.map(forward, column_blocks)
    operator_times_prior = product_blocks.transpose(1, 0, 2).reshape(MATRIX_ORDER, MATRIX_ORDER)
    noise_flat = noise_var.reshape(MATRIX_ORDER)

    def backward(pair):
        s_rows, start = pair
        output_matrix = propagate(s_rows.T.astype(jnp.float32))
        on_diag = jnp.arange(MATRIX_ORDER, dtype=jnp.int32)[:, None] == (start + jnp.arange(width_per_block, dtype=jnp.int32))[None, :]
        return output_matrix + jnp.where(on_diag, noise_flat[:, None], jnp.zeros((), jnp.float32))

    blocks_by_row = operator_times_prior.reshape(count_of_blocks, width_per_block, MATRIX_ORDER)
    starts = jnp.arange(count_of_blocks, dtype=jnp.int32) * width_per_block
    prior_matrix_tiles = lax.map(backward, (blocks_by_row, starts))
    predicted_spread_matrix = prior_matrix_tiles.transpose(1, 0, 2).reshape(MATRIX_ORDER, MATRIX_ORDER)
    return predicted_spread_matrix, operator_times_prior
```

```python
import functools

import jax
import jax.numpy as jnp
from jax import lax
from jax.experimental import pallas as pl
from jax.experimental.pallas import tpu as pltpu
from jax.sharding import PartitionSpec as P

MESH = pl.DeviceIdType.MESH
F32 = jnp.float32
BF16 = jnp.bfloat16
STEPS = 3


def chunk_of(i):
    return jnp.where(i < 2, i + 3, jnp.where(i < 5, i - 2, i))


def put_weights(dst, span, first_lat, nlat, table, diffusivity, index):
    for step in range(STEPS):

        def one(place, carry, step=step):
            lat = first_lat + place
            inside = jnp.where((lat >= 0) & (lat < nlat), 1.0, 0.0).astype(F32)
            regime = index[step, jnp.clip(lat, 0, nlat - 1)]
            zonal, merid, diffuse = table[regime, 0], table[regime, 1], diffusivity[regime]
            zz, mm = 0.5 * zonal * zonal, 0.5 * merid * merid
            at = (step * span + place) * 5
            dst[at] = inside * (1.0 - zonal * zonal - merid * merid - 4.0 * diffuse)
            dst[at + 1] = inside * (zz - 0.5 * zonal + diffuse)
            dst[at + 2] = inside * (zz + 0.5 * zonal + diffuse)
            dst[at + 3] = inside * (mm - 0.5 * merid + diffuse)
            dst[at + 4] = inside * (mm + 0.5 * merid + diffuse)
            return carry

        lax.fori_loop(step + 1, span - 1 - step, one, 0)


def kernel(
    nlat, nrow, ncol,
    cov, noise, table, diffusivity, index,
    out, s_out,
    buf0, buf1, buf2, tt, sb, l2, r2, l1, r1, ob, w_row, w_col,
    load_sem, row_send, row_recv, one_send, one_recv, two_send, two_recv, out_sem, s_sem,
):
    strip, nlon, width = cov.shape
    row, col = lax.axis_index("row"), lax.axis_index("col")
    has_up, has_down = row > 0, row < nrow - 1
    has_left, has_right = col > 0, col < ncol - 1
    up, down = (lax.rem(row + nrow - 1, nrow), col), (lax.rem(row + 1, nrow), col)
    left, right = (row, lax.rem(col + ncol - 1, ncol)), (row, lax.rem(col + 1, ncol))
    span = strip + 2 * STEPS

    load = pltpu.make_async_copy(cov, buf0.at[pl.ds(STEPS, strip)], load_sem)
    load.start()

    barrier = pltpu.get_barrier_semaphore()
    count = 0
    for there, peer in ((has_up, up), (has_down, down), (has_left, left), (has_right, right)):

        @pl.when(there)
        def _(peer=peer):
            pl.semaphore_signal(barrier, inc=1, device_id=peer, device_id_type=MESH)

        count = count + jnp.where(there, 1, 0)

    put_weights(w_row, span, row * strip - STEPS, nlat, table, diffusivity, index)
    put_weights(w_col, 8, col * 2 - STEPS, nlat, table, diffusivity, index)

    @pl.when(jnp.logical_not(has_up))
    def _():
        buf0[pl.ds(0, STEPS)] = jnp.zeros((STEPS, nlon, width), F32)

    @pl.when(jnp.logical_not(has_down))
    def _():
        buf0[pl.ds(strip + STEPS, STEPS)] = jnp.zeros((STEPS, nlon, width), F32)

    @pl.when(jnp.logical_not(has_left))
    def _():
        l2[...] = jnp.zeros(l2.shape, BF16)
        l1[...] = jnp.zeros(l1.shape, BF16)

    @pl.when(jnp.logical_not(has_right))
    def _():
        r2[...] = jnp.zeros(r2.shape, BF16)
        r1[...] = jnp.zeros(r1.shape, BF16)

    pl.semaphore_wait(barrier, count)

    to_up = pltpu.make_async_remote_copy(
        src_ref=cov.at[pl.ds(0, STEPS)], dst_ref=buf0.at[pl.ds(strip + STEPS, STEPS)],
        send_sem=row_send.at[0], recv_sem=row_recv.at[0], device_id=up, device_id_type=MESH,
    )
    to_down = pltpu.make_async_remote_copy(
        src_ref=cov.at[pl.ds(strip - STEPS, STEPS)], dst_ref=buf0.at[pl.ds(0, STEPS)],
        send_sem=row_send.at[1], recv_sem=row_recv.at[1], device_id=down, device_id_type=MESH,
    )

    @pl.when(has_up)
    def _():
        to_up.start()

    @pl.when(has_down)
    def _():
        to_down.start()

    def rows_step(src, dst, step, first, last, base):
        def one(place, carry):
            at = (step * span + place) * 5
            mid, east, west, north, south = (w_row[at + n] for n in range(5))
            for half in range(width // 128):
                lanes = pl.ds(half * 128, 128)
                value = src[place, :, lanes]
                value = (
                    mid * value
                    + east * pltpu.roll(value, nlon - 1, 0)
                    + west * pltpu.roll(value, 1, 0)
                    + north * src[place + 1, :, lanes]
                    + south * src[place - 1, :, lanes]
                )
                dst[place - base, :, lanes] = value
                if step == STEPS - 1:
                    sb[place - base, :, lanes] = value.astype(BF16)
            return carry

        lax.fori_loop(first, last, one, 0)

    def first_message(i, side):
        lat = chunk_of(i)
        return pltpu.make_async_remote_copy(
            src_ref=sb.at[lat], dst_ref=(l2, r2)[side].at[lat],
            send_sem=one_send.at[side, i], recv_sem=one_recv.at[side, i],
            device_id=(right, left)[side], device_id_type=MESH,
        )

    def second_message(i, side):
        lat = chunk_of(i)
        lanes = (pl.ds(128, 128), pl.ds(0, 128))[side]
        return pltpu.make_async_remote_copy(
            src_ref=(l2, r2)[side].at[lat, :, lanes], dst_ref=(l1, r1)[side].at[lat],
            send_sem=two_send.at[side, i], recv_sem=two_recv.at[side, i],
            device_id=(right, left)[side], device_id_type=MESH,
        )

    def store_s(i):
        lat = chunk_of(i)
        return pltpu.make_async_copy(sb.at[lat], s_out.at[lat], s_sem.at[i])

    def store_out(i):
        lat = chunk_of(i)
        return pltpu.make_async_copy(ob.at[lat], out.at[lat], out_sem.at[i])

    def send_first(start, stop):
        def one(i, carry):
            @pl.when(has_right)
            def _():
                first_message(i, 0).start()

            @pl.when(has_left)
            def _():
                first_message(i, 1).start()

            store_s(i).start()
            return carry

        lax.fori_loop(start, stop, one, 0)

    load.wait()
    rows_step(buf0, buf1, 0, 4, 10, 0)
    rows_step(buf1, buf2, 1, 5, 9, 0)
    rows_step(buf2, tt, 2, 6, 8, STEPS)
    send_first(0, 2)

    @pl.when(has_up)
    def _():
        to_down.wait_recv()

    rows_step(buf0, buf1, 0, 1, 4, 0)
    rows_step(buf1, buf2, 1, 2, 5, 0)
    rows_step(buf2, tt, 2, 3, 6, STEPS)
    send_first(2, 5)

    @pl.when(has_down)
    def _():
        to_up.wait_recv()

    rows_step(buf0, buf1, 0, 10, 13, 0)
    rows_step(buf1, buf2, 1, 9, 12, 0)
    rows_step(buf2, tt, 2, 8, 11, STEPS)
    send_first(5, 8)

    def pass_on(i):
        @pl.when(has_left)
        def _():
            first_message(i, 0).wait_recv()

            @pl.when(has_right)
            def _():
                second_message(i, 0).start()

        @pl.when(has_right)
        def _():
            first_message(i, 1).wait_recv()

            @pl.when(has_left)
            def _():
                second_message(i, 1).start()

    def columns(i):
        lat = chunk_of(i)

        @pl.when(col > 1)
        def _():
            second_message(i, 0).wait_recv()

        @pl.when(col < ncol - 2)
        def _():
            second_message(i, 1).wait_recv()

        def one(q, carry):
            rows = pl.ds(pl.multiple_of(q * 16, 16), 16)
            v = [
                l1[lat, rows, :],
                l2[lat, rows, 0:128],
                l2[lat, rows, 128:256],
                tt[lat, rows, 0:128],
                tt[lat, rows, 128:256],
                r2[lat, rows, 0:128],
                r2[lat, rows, 128:256],
                r1[lat, rows, :],
            ]
            v = [x.astype(F32) for x in v]
            for step in range(STEPS):
                fresh = []
                for n in range(1, len(v) - 1):
                    at = (step * 8 + n + step) * 5
                    mid, east, west, north, south = (w_col[at + m] for m in range(5))
                    fresh.append(
                        mid * v[n]
                        + east * pltpu.roll(v[n], 127, 1)
                        + west * pltpu.roll(v[n], 1, 1)
                        + north * v[n + 1]
                        + south * v[n - 1]
                    )
                v = fresh
            ob[lat, rows, 0:128] = v[0]
            ob[lat, rows, 128:256] = v[1]
            return carry

        lax.fori_loop(0, nlon // 16, one, 0)
        for half in range(2):

            @pl.when(row * strip + lat == col * 2 + half)
            def _(half=half):
                lanes = pl.ds(half * 128, 128)
                own = lax.broadcasted_iota(jnp.int32, (128, 128), 0) == lax.broadcasted_iota(
                    jnp.int32, (128, 128), 1
                )
                line = noise[pl.ds(lat, 1), :]
                ob[lat, :, lanes] = ob[lat, :, lanes] + jnp.where(own, line, 0.0)

        store_out(i).start()

    pass_on(0)

    def turn(i, carry):
        @pl.when(i < strip)
        def _():
            pass_on(i)

        columns(i - 1)
        return carry

    lax.fori_loop(1, strip + 1, turn, 0)

    def finish(i, carry):
        store_s(i).wait()
        store_out(i).wait()

        @pl.when(has_right)
        def _():
            first_message(i, 0).wait_send()

        @pl.when(has_left)
        def _():
            first_message(i, 1).wait_send()

        @pl.when(has_left & has_right)
        def _():
            second_message(i, 0).wait_send()
            second_message(i, 1).wait_send()

        return carry

    lax.fori_loop(0, strip, finish, 0)

    @pl.when(has_up)
    def _():
        to_up.wait_send()

    @pl.when(has_down)
    def _():
        to_down.wait_send()


def solution(mesh):
    nrow, ncol = mesh.shape["row"], mesh.shape["col"]

    def body(covariance, noise_var, wind_table, diffusivity, wind_index):
        rows_dev, cols_dev = covariance.shape
        strip, nlon = noise_var.shape
        nlat = wind_index.shape[1]
        block = (strip, nlon, cols_dev)
        half = (strip, nlon, nlon)
        span = (strip + 2 * STEPS, nlon, cols_dev)
        anywhere = pl.BlockSpec(memory_space=pl.ANY)
        scalars = pl.BlockSpec(memory_space=pltpu.SMEM)
        out, s = pl.pallas_call(
            functools.partial(kernel, nlat, nrow, ncol),
            out_shape=(jax.ShapeDtypeStruct(block, F32), jax.ShapeDtypeStruct(block, BF16)),
            in_specs=[anywhere, pl.BlockSpec(memory_space=pltpu.VMEM), scalars, scalars, scalars],
            out_specs=(anywhere, anywhere),
            scratch_shapes=[
                pltpu.VMEM(span, F32),
                pltpu.VMEM(span, F32),
                pltpu.VMEM(span, F32),
                pltpu.VMEM(block, F32),
                pltpu.VMEM(block, BF16),
                pltpu.VMEM(block, BF16),
                pltpu.VMEM(block, BF16),
                pltpu.VMEM(half, BF16),
                pltpu.VMEM(half, BF16),
                pltpu.VMEM(block, F32),
                pltpu.SMEM((STEPS * (strip + 2 * STEPS) * 5,), F32),
                pltpu.SMEM((STEPS * 8 * 5,), F32),
                pltpu.SemaphoreType.DMA,
                pltpu.SemaphoreType.DMA((2,)),
                pltpu.SemaphoreType.DMA((2,)),
                pltpu.SemaphoreType.DMA((2, strip)),
                pltpu.SemaphoreType.DMA((2, strip)),
                pltpu.SemaphoreType.DMA((2, strip)),
                pltpu.SemaphoreType.DMA((2, strip)),
                pltpu.SemaphoreType.DMA((strip,)),
                pltpu.SemaphoreType.DMA((strip,)),
            ],
            compiler_params=pltpu.CompilerParams(collective_id=0, has_side_effects=True),
        )(covariance.reshape(block), noise_var, wind_table, diffusivity, wind_index)
        return out.reshape(rows_dev, cols_dev), s.reshape(rows_dev, cols_dev)

    in_specs = (P("row", "col"), P("row", None), P(), P(), P())
    out_specs = (P("row", "col"), P("row", "col"))
    return jax.shard_map(body, mesh=mesh, in_specs=in_specs, out_specs=out_specs, check_vma=False)
```

```python
import functools

import jax
import jax.numpy as jnp
from jax import lax
from jax.experimental import pallas as pl
from jax.experimental.pallas import tpu as pltpu
from jax.sharding import PartitionSpec as P

MESH = pl.DeviceIdType.MESH
F32 = jnp.float32
BF16 = jnp.bfloat16
STEPS = 3
AHEAD = 3


def chunk_of(i):
    return jnp.where(i < 2, i + 3, jnp.where(i < 5, i - 2, i))


def put_weights(dst, span, first_lat, nlat, table, diffusivity, index):
    for step in range(STEPS):

        def one(place, carry, step=step):
            lat = first_lat + place
            inside = jnp.where((lat >= 0) & (lat < nlat), 1.0, 0.0).astype(F32)
            regime = index[step, jnp.clip(lat, 0, nlat - 1)]
            zonal, merid, diffuse = table[0, regime], table[1, regime], diffusivity[regime]
            zz, mm = 0.5 * zonal * zonal, 0.5 * merid * merid
            at = (step * span + place) * 5
            dst[at] = inside * (1.0 - zonal * zonal - merid * merid - 4.0 * diffuse)
            dst[at + 1] = inside * (zz - 0.5 * zonal + diffuse)
            dst[at + 2] = inside * (zz + 0.5 * zonal + diffuse)
            dst[at + 3] = inside * (mm - 0.5 * merid + diffuse)
            dst[at + 4] = inside * (mm + 0.5 * merid + diffuse)
            return carry

        lax.fori_loop(step + 1, span - 1 - step, one, 0)


def kernel(
    nlat, nrow, ncol,
    cov, noise, table, diffusivity, index,
    ob, sb,
    buf0, buf1, buf2, low, l2, r2, far, held, w_high, w_low, w_row, w_col,
    load_sem, row_send, row_recv, one_send, one_recv, two_send, two_recv, held_send, held_recv,
):
    strip, nlon, width = cov.shape
    row, col = lax.axis_index("row"), lax.axis_index("col")
    has_up, has_down = row > 0, row < nrow - 1
    has_left, has_right = col > 0, col < ncol - 1
    up, down = (lax.rem(row + nrow - 1, nrow), col), (lax.rem(row + 1, nrow), col)
    left, right = (row, lax.rem(col + ncol - 1, ncol)), (row, lax.rem(col + 1, ncol))
    span = strip + 2 * STEPS

    edge = ncol // 2 - 1
    near_relay = (col == edge - 3) | (col == edge + 4)
    far_relay = (col == 0) | (col == ncol - 1)
    relays = near_relay | far_relay
    at_edge = (col == edge) | (col == edge + 1)
    lower = col <= edge
    relay_from = jnp.where(lower, edge, edge + 1)
    relay_to = jnp.where(lower, edge + 1, edge)

    load = pltpu.make_async_copy(cov, buf0.at[pl.ds(STEPS, strip)], load_sem)
    load.start()

    barrier = pltpu.get_barrier_semaphore()

    @pl.when(at_edge)
    def _():
        for peer in (jnp.where(lower, edge + 4, 0), jnp.where(lower, ncol - 1, edge - 3)):
            pl.semaphore_signal(barrier, inc=1, device_id=(row, peer), device_id_type=MESH)

    @pl.when(relays)
    def _():
        pl.semaphore_signal(barrier, inc=1, device_id=(row, relay_from), device_id_type=MESH)

    count = jnp.where(at_edge, 2, 0) + jnp.where(relays, 1, 0)
    for there, peer in ((has_up, up), (has_down, down), (has_left, left), (has_right, right)):

        @pl.when(there)
        def _(peer=peer):
            pl.semaphore_signal(barrier, inc=1, device_id=peer, device_id_type=MESH)

        count = count + jnp.where(there, 1, 0)

    put_weights(w_row, span, row * strip - STEPS, nlat, table, diffusivity, index)
    put_weights(w_col, 8, col * 2 - STEPS, nlat, table, diffusivity, index)

    @pl.when(jnp.logical_not(has_up))
    def _():
        buf0[pl.ds(0, STEPS)] = jnp.zeros((STEPS, nlon, width), F32)

    @pl.when(jnp.logical_not(has_down))
    def _():
        buf0[pl.ds(strip + STEPS, STEPS)] = jnp.zeros((STEPS, nlon, width), F32)

    @pl.when(jnp.logical_not(has_left))
    def _():
        l2[...] = jnp.zeros(l2.shape, BF16)

    @pl.when(jnp.logical_not(has_right))
    def _():
        r2[...] = jnp.zeros(r2.shape, BF16)

    @pl.when(col <= 1)
    def _():
        far[:, :, 0:128] = jnp.zeros((strip, nlon, 128), BF16)

    @pl.when(col >= ncol - 2)
    def _():
        far[:, :, 128:256] = jnp.zeros((strip, nlon, 128), BF16)

    sub = lax.broadcasted_iota(jnp.int32, (8, 128), 0)
    middle = lax.broadcasted_iota(jnp.int32, (8, 128), 1) == 64
    v = [jnp.where((sub == n) & middle, 1.0, 0.0).astype(F32) for n in range(8)]
    for step in range(STEPS):
        fresh = []
        for n in range(1, len(v) - 1):
            at = (step * 8 + n + step) * 5
            mid, east, west, north, south = (w_col[at + m] for m in range(5))
            fresh.append(
                mid * v[n]
                + east * pltpu.roll(v[n], 127, 1)
                + west * pltpu.roll(v[n], 1, 1)
                + north * v[n + 1]
                + south * v[n - 1]
            )
        v = fresh
    for place, lat in enumerate((0, 7, 1, 2, 3, 4, 5, 6)):
        for half in range(2):
            line = jnp.broadcast_to(v[half][lat : lat + 1, :], (128, 128))
            block = pltpu.roll(line, 64, 1, stride=1, stride_axis=0)
            rows, lanes = pl.ds((place % 2) * 128, 128), pl.ds(half * 128, 128)
            high = block.astype(BF16)
            w_high[place // 2, rows, lanes] = high
            w_low[place // 2, rows, lanes] = (block - high.astype(F32)).astype(BF16)

    pl.semaphore_wait(barrier, count)

    to_up = pltpu.make_async_remote_copy(
        src_ref=cov.at[pl.ds(0, STEPS)], dst_ref=buf0.at[pl.ds(strip + STEPS, STEPS)],
        send_sem=row_send.at[0], recv_sem=row_recv.at[0], device_id=up, device_id_type=MESH,
    )
    to_down = pltpu.make_async_remote_copy(
        src_ref=cov.at[pl.ds(strip - STEPS, STEPS)], dst_ref=buf0.at[pl.ds(0, STEPS)],
        send_sem=row_send.at[1], recv_sem=row_recv.at[1], device_id=down, device_id_type=MESH,
    )

    @pl.when(has_up)
    def _():
        to_up.start()

    @pl.when(has_down)
    def _():
        to_down.start()

    def rows_step(src, dst, step, first, last, base):
        def one(place, carry):
            at = (step * span + place) * 5
            mid, east, west, north, south = (w_row[at + n] for n in range(5))
            for half in range(width // 128):
                lanes = pl.ds(half * 128, 128)
                value = src[place, :, lanes]
                value = (
                    mid * value
                    + east * pltpu.roll(value, nlon - 1, 0)
                    + west * pltpu.roll(value, 1, 0)
                    + north * src[place + 1, :, lanes]
                    + south * src[place - 1, :, lanes]
                )
                if step < STEPS - 1:
                    dst[place - base, :, lanes] = value
                else:
                    high = value.astype(BF16)
                    sb[place - base, :, lanes] = high
                    dst[place - base, :, lanes] = (value - high.astype(F32)).astype(BF16)
            return carry

        lax.fori_loop(first, last, one, 0)

    def first_message(i, side):
        lat = chunk_of(i)
        return pltpu.make_async_remote_copy(
            src_ref=sb.at[lat], dst_ref=(l2, r2)[side].at[lat],
            send_sem=one_send.at[side, i], recv_sem=one_recv.at[side, i],
            device_id=(right, left)[side], device_id_type=MESH,
        )

    def to_relay(i, side):
        near, away = ((edge - 3, 0), (edge + 4, ncol - 1))[side]
        return pltpu.make_async_remote_copy(
            src_ref=sb.at[chunk_of(i)], dst_ref=held.at[i // 2],
            send_sem=one_send.at[side, i], recv_sem=held_recv.at[i // 2],
            device_id=(row, jnp.where(lax.rem(i, 2) == 0, near, away)), device_id_type=MESH,
        )

    def from_relay(j, side):
        i = 2 * j + jnp.where(near_relay, 0, 1)
        return pltpu.make_async_remote_copy(
            src_ref=held.at[j], dst_ref=(l2, r2)[side].at[chunk_of(i)],
            send_sem=held_send.at[j], recv_sem=one_recv.at[side, i],
            device_id=(row, relay_to), device_id_type=MESH,
        )

    def second_message(i, side):
        lat = chunk_of(i)
        lanes = (pl.ds(128, 128), pl.ds(0, 128))[side]
        return pltpu.make_async_remote_copy(
            src_ref=(l2, r2)[side].at[lat, :, lanes],
            dst_ref=far.at[lat, :, pl.ds(side * 128, 128)],
            send_sem=two_send.at[side, i], recv_sem=two_recv.at[side, i],
            device_id=(right, left)[side], device_id_type=MESH,
        )

    def send_first(start, stop):
        def one(i, carry):
            @pl.when(has_right & (col != edge))
            def _():
                first_message(i, 0).start()

            @pl.when(col == edge)
            def _():
                to_relay(i, 0).start()

            @pl.when(has_left & (col != edge + 1))
            def _():
                first_message(i, 1).start()

            @pl.when(col == edge + 1)
            def _():
                to_relay(i, 1).start()

            return carry

        lax.fori_loop(start, stop, one, 0)

    load.wait()
    rows_step(buf0, buf1, 0, 4, 10, 0)
    rows_step(buf1, buf2, 1, 5, 9, 0)
    rows_step(buf2, low, 2, 6, 8, STEPS)
    send_first(0, 2)

    @pl.when(has_up)
    def _():
        to_down.wait_recv()

    rows_step(buf0, buf1, 0, 1, 4, 0)
    rows_step(buf1, buf2, 1, 2, 5, 0)
    rows_step(buf2, low, 2, 3, 6, STEPS)
    send_first(2, 5)

    @pl.when(has_down)
    def _():
        to_up.wait_recv()

    rows_step(buf0, buf1, 0, 10, 13, 0)
    rows_step(buf1, buf2, 1, 9, 12, 0)
    rows_step(buf2, low, 2, 8, 11, STEPS)
    send_first(5, 8)

    def pass_on(i):
        @pl.when(has_left)
        def _():
            first_message(i, 0).wait_recv()

            @pl.when(has_right)
            def _():
                second_message(i, 0).start()

        @pl.when(has_right)
        def _():
            first_message(i, 1).wait_recv()

            @pl.when(has_left)
            def _():
                second_message(i, 1).start()

    def columns(i):
        lat = chunk_of(i)

        @pl.when(col > 1)
        def _():
            second_message(i, 0).wait_recv()

        @pl.when(col < ncol - 2)
        def _():
            second_message(i, 1).wait_recv()

        def dot(x, w):
            return jnp.dot(x, w, preferred_element_type=F32)

        total = dot(low[lat], w_high[2])
        for place, ref in enumerate((far, l2, sb, r2)):
            x = ref[lat]
            total = total + dot(x, w_high[place]) + dot(x, w_low[place])
        ob[lat] = total
        for half in range(2):

            @pl.when(row * strip + lat == col * 2 + half)
            def _(half=half):
                lanes = pl.ds(half * 128, 128)
                own = lax.broadcasted_iota(jnp.int32, (128, 128), 0) == lax.broadcasted_iota(
                    jnp.int32, (128, 128), 1
                )
                line = noise[pl.ds(lat, 1), :]
                ob[lat, :, lanes] = ob[lat, :, lanes] + jnp.where(own, line, 0.0)

    def turn(i, carry):
        @pl.when(i < strip)
        def _():
            pass_on(i)

        @pl.when(relays & (i < strip) & (lax.rem(i, 2) == 1))
        def _():
            j = i // 2

            @pl.when(lower)
            def _():
                to_relay(2 * j, 0).wait_recv()
                from_relay(j, 0).start()

            @pl.when(jnp.logical_not(lower))
            def _():
                to_relay(2 * j, 1).wait_recv()
                from_relay(j, 1).start()

        @pl.when(i >= AHEAD)
        def _():
            columns(i - AHEAD)

        return carry

    lax.fori_loop(0, strip + AHEAD, turn, 0)

    def finish(i, carry):
        @pl.when(has_right)
        def _():
            first_message(i, 0).wait_send()

        @pl.when(has_left)
        def _():
            first_message(i, 1).wait_send()

        @pl.when(has_left & has_right)
        def _():
            second_message(i, 0).wait_send()
            second_message(i, 1).wait_send()

        return carry

    lax.fori_loop(0, strip, finish, 0)

    @pl.when(relays)
    def _():
        for j in range(strip // 2):
            from_relay(j, 0).wait_send()


    @pl.when(has_up)
    def _():
        to_up.wait_send()

    @pl.when(has_down)
    def _():
        to_down.wait_send()


def solution(mesh):
    nrow, ncol = mesh.shape["row"], mesh.shape["col"]

    def body(covariance, noise_var, wind_table, diffusivity, wind_index):
        rows_dev, cols_dev = covariance.shape
        strip, nlon = noise_var.shape
        nlat = wind_index.shape[1]
        block = (strip, nlon, cols_dev)
        span = (strip + 2 * STEPS, nlon, cols_dev)
        anywhere = pl.BlockSpec(memory_space=pltpu.HBM)
        scalars = pl.BlockSpec(memory_space=pltpu.SMEM)
        out, s = pl.pallas_call(
            functools.partial(kernel, nlat, nrow, ncol),
            out_shape=(jax.ShapeDtypeStruct(block, F32), jax.ShapeDtypeStruct(block, BF16)),
            in_specs=[anywhere, pl.BlockSpec(memory_space=pltpu.VMEM), scalars, scalars, scalars],
            out_specs=(pl.BlockSpec(memory_space=pltpu.VMEM),) * 2,
            scratch_shapes=[
                pltpu.VMEM(span, F32),
                pltpu.VMEM(span, F32),
                pltpu.VMEM(span, F32),
                pltpu.VMEM(block, BF16),
                pltpu.VMEM(block, BF16),
                pltpu.VMEM(block, BF16),
                pltpu.VMEM(block, BF16),
                pltpu.VMEM((strip // 2, nlon, cols_dev), BF16),
                pltpu.VMEM((4, 256, 256), BF16),
                pltpu.VMEM((4, 256, 256), BF16),
                pltpu.SMEM((STEPS * (strip + 2 * STEPS) * 5,), F32),
                pltpu.SMEM((STEPS * 8 * 5,), F32),
                pltpu.SemaphoreType.DMA,
                pltpu.SemaphoreType.DMA((2,)),
                pltpu.SemaphoreType.DMA((2,)),
                pltpu.SemaphoreType.DMA((2, strip)),
                pltpu.SemaphoreType.DMA((2, strip)),
                pltpu.SemaphoreType.DMA((2, strip)),
                pltpu.SemaphoreType.DMA((2, strip)),
                pltpu.SemaphoreType.DMA((strip // 2,)),
                pltpu.SemaphoreType.DMA((strip // 2,)),
            ],
            compiler_params=pltpu.CompilerParams(collective_id=0, has_side_effects=True, vmem_limit_bytes=14 << 20),
        )(covariance.reshape(block), noise_var, wind_table.T, diffusivity, wind_index)
        return out.reshape(rows_dev, cols_dev), s.reshape(rows_dev, cols_dev)

    in_specs = (P("row", "col"), P("row", None), P(), P(), P())
    out_specs = (P("row", "col"), P("row", "col"))
    return jax.shard_map(body, mesh=mesh, in_specs=in_specs, out_specs=out_specs, check_vma=False)
```

```python
import functools

import jax
import jax.numpy as jnp
from jax import lax
from jax.experimental import pallas as pl
from jax.experimental.pallas import tpu as pltpu
from jax.sharding import PartitionSpec as P

MESH = pl.DeviceIdType.MESH
F32 = jnp.float32
BF16 = jnp.bfloat16
STEPS = 3


def chunk_of(i):
    even = lax.rem(lax.axis_index("row"), 2) == 0
    return jnp.where(i < 2, i + 3, jnp.where(even, jnp.where(i < 5, i + 3, i - 5), jnp.where(i < 5, i - 2, i)))


def put_weights(dst, span, first_lat, nlat, table, diffusivity, index):
    for step in range(STEPS):

        def one(place, carry, step=step):
            lat = first_lat + place
            inside = jnp.where((lat >= 0) & (lat < nlat), 1.0, 0.0).astype(F32)
            regime = index[step, jnp.clip(lat, 0, nlat - 1)]
            zonal, merid, diffuse = table[0, regime], table[1, regime], diffusivity[regime]
            zz, mm = 0.5 * zonal * zonal, 0.5 * merid * merid
            at = (step * span + place) * 5
            dst[at] = inside * (1.0 - zonal * zonal - merid * merid - 4.0 * diffuse)
            dst[at + 1] = inside * (zz - 0.5 * zonal + diffuse)
            dst[at + 2] = inside * (zz + 0.5 * zonal + diffuse)
            dst[at + 3] = inside * (mm - 0.5 * merid + diffuse)
            dst[at + 4] = inside * (mm + 0.5 * merid + diffuse)
            return carry

        lax.fori_loop(step + 1, span - 1 - step, one, 0)


def kernel(
    nlat, nrow, ncol,
    cov, noise, table, diffusivity, index,
    ob, sb,
    buf0, buf1, buf2, low, l2, r2, far, held, held_far, w_high, w_low, w_row, w_col,
    load_sem, row_send, row_recv, one_send, one_recv, two_send, two_recv, held_send, held_recv, far_send, far_recv,
):
    strip, nlon, width = cov.shape
    row, col = lax.axis_index("row"), lax.axis_index("col")
    has_up, has_down = row > 0, row < nrow - 1
    has_left, has_right = col > 0, col < ncol - 1
    next_left, next_right = has_left & (col != ncol // 2), has_right & (col != ncol // 2 - 1)
    up, down = (lax.rem(row + nrow - 1, nrow), col), (lax.rem(row + 1, nrow), col)
    left, right = (row, lax.rem(col + ncol - 1, ncol)), (row, lax.rem(col + 1, ncol))
    span = strip + 2 * STEPS

    edge = ncol // 2 - 1
    near_relay = (col == 3) | (col == ncol - 4)
    far_relay = (col == 0) | (col == ncol - 1)
    pass_relay = (col == 7) | (col == ncol - 8)
    relays = near_relay | far_relay
    at_edge = (col == edge) | (col == edge + 1)
    lower = col <= edge
    relay_from = jnp.where(lower, edge, edge + 1)
    relay_to = jnp.where(lower, edge + 1, edge)

    load = pltpu.make_async_copy(cov, buf0.at[pl.ds(STEPS, strip)], load_sem)
    load.start()

    barrier = pltpu.get_barrier_semaphore()

    @pl.when(at_edge)
    def _():
        for peer in (
            jnp.where(lower, ncol - 4, 0),
            jnp.where(lower, ncol - 1, 3),
            jnp.where(lower, ncol - 8, 7),
        ):
            pl.semaphore_signal(barrier, inc=1, device_id=(row, peer), device_id_type=MESH)

    @pl.when(relays | pass_relay)
    def _():
        pl.semaphore_signal(barrier, inc=1, device_id=(row, relay_from), device_id_type=MESH)

    count = jnp.where(at_edge, 3, 0) + jnp.where(relays | pass_relay, 1, 0)
    for there, peer in ((has_up, up), (has_down, down), (next_left, left), (next_right, right)):

        @pl.when(there)
        def _(peer=peer):
            pl.semaphore_signal(barrier, inc=1, device_id=peer, device_id_type=MESH)

        count = count + jnp.where(there, 1, 0)

    put_weights(w_row, span, row * strip - STEPS, nlat, table, diffusivity, index)
    put_weights(w_col, 8, col * 2 - STEPS, nlat, table, diffusivity, index)

    @pl.when(jnp.logical_not(has_up))
    def _():
        buf0[pl.ds(0, STEPS)] = jnp.zeros((STEPS, nlon, width), F32)

    @pl.when(jnp.logical_not(has_down))
    def _():
        buf0[pl.ds(strip + STEPS, STEPS)] = jnp.zeros((STEPS, nlon, width), F32)

    @pl.when(jnp.logical_not(has_left))
    def _():
        l2[...] = jnp.zeros(l2.shape, BF16)

    @pl.when(jnp.logical_not(has_right))
    def _():
        r2[...] = jnp.zeros(r2.shape, BF16)

    @pl.when(col <= 1)
    def _():
        far[:, :, 0:128] = jnp.zeros((strip, nlon, 128), BF16)

    @pl.when(col >= ncol - 2)
    def _():
        far[:, :, 128:256] = jnp.zeros((strip, nlon, 128), BF16)

    sub = lax.broadcasted_iota(jnp.int32, (8, 128), 0)
    middle = lax.broadcasted_iota(jnp.int32, (8, 128), 1) == 64
    v = [jnp.where((sub == n) & middle, 1.0, 0.0).astype(F32) for n in range(8)]
    for step in range(STEPS):
        fresh = []
        for n in range(1, len(v) - 1):
            at = (step * 8 + n + step) * 5
            mid, east, west, north, south = (w_col[at + m] for m in range(5))
            fresh.append(
                mid * v[n]
                + east * pltpu.roll(v[n], 127, 1)
                + west * pltpu.roll(v[n], 1, 1)
                + north * v[n + 1]
                + south * v[n - 1]
            )
        v = fresh
    for place, lat in enumerate((0, 7, 1, 2, 3, 4, 5, 6)):
        for half in range(2):
            line = jnp.broadcast_to(v[half][lat : lat + 1, :], (128, 128))
            block = pltpu.roll(line, 64, 1, stride=1, stride_axis=0)
            rows, lanes = pl.ds((place % 2) * 128, 128), pl.ds(half * 128, 128)
            high = block.astype(BF16)
            w_high[place // 2, rows, lanes] = high
            w_low[place // 2, rows, lanes] = (block - high.astype(F32)).astype(BF16)

    pl.semaphore_wait(barrier, count)

    to_up = pltpu.make_async_remote_copy(
        src_ref=cov.at[pl.ds(0, STEPS)], dst_ref=buf0.at[pl.ds(strip + STEPS, STEPS)],
        send_sem=row_send.at[0], recv_sem=row_recv.at[0], device_id=up, device_id_type=MESH,
    )
    to_down = pltpu.make_async_remote_copy(
        src_ref=cov.at[pl.ds(strip - STEPS, STEPS)], dst_ref=buf0.at[pl.ds(0, STEPS)],
        send_sem=row_send.at[1], recv_sem=row_recv.at[1], device_id=down, device_id_type=MESH,
    )

    @pl.when(has_up)
    def _():
        to_up.start()

    @pl.when(has_down)
    def _():
        to_down.start()

    def rows_step(src, dst, step, first, last, base):
        def one(place, carry):
            at = (step * span + place) * 5
            mid, east, west, north, south = (w_row[at + n] for n in range(5))
            for half in range(width // 128):
                lanes = pl.ds(half * 128, 128)
                value = src[place, :, lanes]
                value = (
                    mid * value
                    + east * pltpu.roll(value, nlon - 1, 0)
                    + west * pltpu.roll(value, 1, 0)
                    + north * src[place + 1, :, lanes]
                    + south * src[place - 1, :, lanes]
                )
                if step < STEPS - 1:
                    dst[place - base, :, lanes] = value
                else:
                    high = value.astype(BF16)
                    sb[place - base, :, lanes] = high
                    dst[place - base, :, lanes] = (value - high.astype(F32)).astype(BF16)
            return carry

        lax.fori_loop(first, last, one, 0)

    def first_message(i, side):
        lat = chunk_of(i)
        return pltpu.make_async_remote_copy(
            src_ref=sb.at[lat], dst_ref=(l2, r2)[side].at[lat],
            send_sem=one_send.at[side, i], recv_sem=one_recv.at[side, i],
            device_id=(right, left)[side], device_id_type=MESH,
        )

    def to_relay(i, side):
        near, away = ((3, 0), (ncol - 4, ncol - 1))[side]
        return pltpu.make_async_remote_copy(
            src_ref=sb.at[chunk_of(i)], dst_ref=held.at[i // 2],
            send_sem=one_send.at[side, i], recv_sem=held_recv.at[i // 2],
            device_id=(row, jnp.where(lax.rem(i, 2) == 0, near, away)), device_id_type=MESH,
        )

    def from_relay(j, side):
        i = 2 * j + jnp.where(near_relay, 0, 1)
        return pltpu.make_async_remote_copy(
            src_ref=held.at[j], dst_ref=(l2, r2)[side].at[chunk_of(i)],
            send_sem=held_send.at[j], recv_sem=one_recv.at[side, i],
            device_id=(row, relay_to), device_id_type=MESH,
        )

    def second_message(i, side):
        lat = chunk_of(i)
        lanes = (pl.ds(128, 128), pl.ds(0, 128))[side]
        return pltpu.make_async_remote_copy(
            src_ref=(l2, r2)[side].at[lat, :, lanes],
            dst_ref=far.at[lat, :, pl.ds(side * 128, 128)],
            send_sem=two_send.at[side, i], recv_sem=two_recv.at[side, i],
            device_id=(right, left)[side], device_id_type=MESH,
        )

    def send_first(start, stop):
        def one(i, carry):
            @pl.when(has_right & (col != edge))
            def _():
                first_message(i, 0).start()

            @pl.when(col == edge)
            def _():
                to_relay(i, 0).start()

            @pl.when(has_left & (col != edge + 1))
            def _():
                first_message(i, 1).start()

            @pl.when(col == edge + 1)
            def _():
                to_relay(i, 1).start()

            return carry

        lax.fori_loop(start, stop, one, 0)

    load.wait()
    rows_step(buf0, buf1, 0, 4, 10, 0)
    rows_step(buf1, buf2, 1, 5, 9, 0)
    rows_step(buf2, low, 2, 6, 8, STEPS)
    send_first(0, 2)

    def end_rows(bottom):
        @pl.when(jnp.logical_not(bottom) & has_up)
        def _():
            to_down.wait_recv()

        @pl.when(bottom & has_down)
        def _():
            to_up.wait_recv()

        for src, dst, step, top_first, bottom_first, base in (
            (buf0, buf1, 0, 1, strip + 2, 0),
            (buf1, buf2, 1, 2, strip + 1, 0),
            (buf2, low, 2, 3, strip, STEPS),
        ):
            first = jnp.where(bottom, bottom_first, top_first)
            rows_step(src, dst, step, first, first + STEPS, base)

    even = lax.rem(row, 2) == 0
    end_rows(even)
    send_first(2, 5)
    end_rows(jnp.logical_not(even))
    send_first(5, 8)

    def pass_to_relay(i, side):
        lanes = (pl.ds(128, 128), pl.ds(0, 128))[side]
        return pltpu.make_async_remote_copy(
            src_ref=(l2, r2)[side].at[chunk_of(i), :, lanes], dst_ref=held_far.at[i],
            send_sem=two_send.at[side, i], recv_sem=far_recv.at[i],
            device_id=(row, (7, ncol - 8)[side]), device_id_type=MESH,
        )

    def pass_from_relay(i, side):
        return pltpu.make_async_remote_copy(
            src_ref=held_far.at[i], dst_ref=far.at[chunk_of(i), :, pl.ds(side * 128, 128)],
            send_sem=far_send.at[i], recv_sem=two_recv.at[side, i],
            device_id=(row, relay_to), device_id_type=MESH,
        )

    def pass_on(i, side, there, onward):
        @pl.when(there)
        def _():
            first_message(i, side).wait_recv()

            @pl.when(onward)
            def _():
                second_message(i, side).start()

            @pl.when(col == edge + side)
            def _():
                pass_to_relay(i, side).start()

    def columns(i):
        lat = chunk_of(i)

        @pl.when(col > 1)
        def _():
            second_message(i, 0).wait_recv()

        @pl.when(col < ncol - 2)
        def _():
            second_message(i, 1).wait_recv()

        def dot(x, w):
            return jnp.dot(x, w, preferred_element_type=F32)

        total = dot(low[lat], w_high[2])
        for place, ref in enumerate((far, l2, sb, r2)):
            x = ref[lat]
            total = total + dot(x, w_high[place]) + dot(x, w_low[place])
        ob[lat] = total
        for half in range(2):

            @pl.when(row * strip + lat == col * 2 + half)
            def _(half=half):
                lanes = pl.ds(half * 128, 128)
                own = lax.broadcasted_iota(jnp.int32, (128, 128), 0) == lax.broadcasted_iota(
                    jnp.int32, (128, 128), 1
                )
                line = noise[pl.ds(lat, 1), :]
                ob[lat, :, lanes] = ob[lat, :, lanes] + jnp.where(own, line, 0.0)

    def turn(i, carry):
        for side, here in ((0, lower), (1, jnp.logical_not(lower))):

            @pl.when(here & ((near_relay & (lax.rem(i, 2) == 0)) | (far_relay & (lax.rem(i, 2) == 1))))
            def _(side=side):
                to_relay(i, side).wait_recv()
                from_relay(i // 2, side).start()

        pass_on(i, 0, next_left, next_right)
        pass_on(i, 1, next_right, next_left)
        for side, here in ((0, lower), (1, jnp.logical_not(lower))):

            @pl.when(here & pass_relay & (i > 0))
            def _(side=side):
                pass_to_relay(i - 1, side).wait_recv()
                pass_from_relay(i - 1, side).start()

        return carry

    lax.fori_loop(0, strip, turn, 0)
    for side, here in ((0, lower), (1, jnp.logical_not(lower))):

        @pl.when(here & pass_relay)
        def _(side=side):
            pass_to_relay(strip - 1, side).wait_recv()
            pass_from_relay(strip - 1, side).start()

    def last_turn(i, carry):
        pass_on(i, 0, col == edge + 1, True)
        pass_on(i, 1, col == edge, True)
        columns(i)
        return carry

    lax.fori_loop(0, strip, last_turn, 0)

    def finish(i, carry):
        @pl.when(has_right)
        def _():
            first_message(i, 0).wait_send()

        @pl.when(has_left)
        def _():
            first_message(i, 1).wait_send()

        @pl.when(has_left & has_right)
        def _():
            second_message(i, 0).wait_send()
            second_message(i, 1).wait_send()

        return carry

    lax.fori_loop(0, strip, finish, 0)

    @pl.when(relays)
    def _():
        for j in range(strip // 2):
            from_relay(j, 0).wait_send()

    @pl.when(pass_relay)
    def _():
        for i in range(strip):
            pass_from_relay(i, 0).wait_send()


    @pl.when(has_up)
    def _():
        to_up.wait_send()

    @pl.when(has_down)
    def _():
        to_down.wait_send()


def solution(mesh):
    nrow, ncol = mesh.shape["row"], mesh.shape["col"]

    def body(covariance, noise_var, wind_table, diffusivity, wind_index):
        rows_dev, cols_dev = covariance.shape
        strip, nlon = noise_var.shape
        nlat = wind_index.shape[1]
        block = (strip, nlon, cols_dev)
        span = (strip + 2 * STEPS, nlon, cols_dev)
        anywhere = pl.BlockSpec(memory_space=pltpu.HBM)
        scalars = pl.BlockSpec(memory_space=pltpu.SMEM)
        out, s = pl.pallas_call(
            functools.partial(kernel, nlat, nrow, ncol),
            out_shape=(jax.ShapeDtypeStruct(block, F32), jax.ShapeDtypeStruct(block, BF16)),
            in_specs=[anywhere, pl.BlockSpec(memory_space=pltpu.VMEM), scalars, scalars, scalars],
            out_specs=(pl.BlockSpec(memory_space=pltpu.VMEM),) * 2,
            scratch_shapes=[
                pltpu.VMEM(span, F32),
                pltpu.VMEM(span, F32),
                pltpu.VMEM(span, F32),
                pltpu.VMEM(block, BF16),
                pltpu.VMEM(block, BF16),
                pltpu.VMEM(block, BF16),
                pltpu.VMEM(block, BF16),
                pltpu.VMEM((strip // 2, nlon, cols_dev), BF16),
                pltpu.VMEM((strip, nlon, nlon), BF16),
                pltpu.VMEM((4, 256, 256), BF16),
                pltpu.VMEM((4, 256, 256), BF16),
                pltpu.SMEM((STEPS * (strip + 2 * STEPS) * 5,), F32),
                pltpu.SMEM((STEPS * 8 * 5,), F32),
                pltpu.SemaphoreType.DMA,
                pltpu.SemaphoreType.DMA((2,)),
                pltpu.SemaphoreType.DMA((2,)),
                pltpu.SemaphoreType.DMA((2, strip)),
                pltpu.SemaphoreType.DMA((2, strip)),
                pltpu.SemaphoreType.DMA((2, strip)),
                pltpu.SemaphoreType.DMA((2, strip)),
                pltpu.SemaphoreType.DMA((strip // 2,)),
                pltpu.SemaphoreType.DMA((strip // 2,)),
                pltpu.SemaphoreType.DMA((strip,)),
                pltpu.SemaphoreType.DMA((strip,)),
            ],
            compiler_params=pltpu.CompilerParams(collective_id=0, has_side_effects=True, vmem_limit_bytes=54755328),
        )(covariance.reshape(block), noise_var, wind_table.T, diffusivity, wind_index)
        return out.reshape(rows_dev, cols_dev), s.reshape(rows_dev, cols_dev)

    in_specs = (P("row", "col"), P("row", None), P(), P(), P())
    out_specs = (P("row", "col"), P("row", "col"))
    return jax.shard_map(body, mesh=mesh, in_specs=in_specs, out_specs=out_specs, check_vma=False)
```

```python
import functools

import jax
import jax.numpy as jnp
from jax import lax
from jax.experimental import pallas as pl
from jax.experimental.pallas import tpu as pltpu
from jax.sharding import PartitionSpec as P

MESH = pl.DeviceIdType.MESH
F32 = jnp.float32
BF16 = jnp.bfloat16
STEPS = 3


def chunk_of(i):
    even = lax.rem(lax.axis_index("row"), 2) == 0
    return jnp.where(i < 2, i + 3, jnp.where(even, jnp.where(i < 5, i + 3, i - 5), jnp.where(i < 5, i - 2, i)))


def put_weights(dst, table, diffusivity):
    for regime in range(diffusivity.shape[0]):
        zonal, merid, diffuse = table[0, regime], table[1, regime], diffusivity[regime]
        zz, mm = 0.5 * zonal * zonal, 0.5 * merid * merid
        dst[regime * 5] = 1.0 - zonal * zonal - merid * merid - 4.0 * diffuse
        dst[regime * 5 + 1] = zz - 0.5 * zonal + diffuse
        dst[regime * 5 + 2] = zz + 0.5 * zonal + diffuse
        dst[regime * 5 + 3] = mm - 0.5 * merid + diffuse
        dst[regime * 5 + 4] = mm + 0.5 * merid + diffuse


def weights_at(weights, index, step, lat):
    nlat = index.shape[1]
    inside = jnp.where((lat >= 0) & (lat < nlat), 1.0, 0.0).astype(F32)
    at = index[step, jnp.clip(lat, 0, nlat - 1)] * 5
    return [inside * weights[at + n] for n in range(5)]


def kernel(
    nlat, nrow, ncol,
    cov, noise, table, diffusivity, index,
    ob, sb,
    buf0, buf1, buf2, low, l2, r2, far, held, held_far, w_high, w_low, weights,
    load_sem, row_send, row_recv, one_send, one_recv, two_send, two_recv, held_send, held_recv, far_send, far_recv,
):
    strip, nlon, width = cov.shape
    row, col = lax.axis_index("row"), lax.axis_index("col")
    has_up, has_down = row > 0, row < nrow - 1
    has_left, has_right = col > 0, col < ncol - 1
    next_left, next_right = has_left & (col != ncol // 2), has_right & (col != ncol // 2 - 1)
    up, down = (lax.rem(row + nrow - 1, nrow), col), (lax.rem(row + 1, nrow), col)
    left, right = (row, lax.rem(col + ncol - 1, ncol)), (row, lax.rem(col + 1, ncol))

    edge = ncol // 2 - 1
    near_relay = (col == 3) | (col == ncol - 4)
    far_relay = (col == 0) | (col == ncol - 1)
    pass_relay = (col == 7) | (col == ncol - 8)
    relays = near_relay | far_relay
    at_edge = (col == edge) | (col == edge + 1)
    lower = col <= edge
    relay_from = jnp.where(lower, edge, edge + 1)
    relay_to = jnp.where(lower, edge + 1, edge)

    load = pltpu.make_async_copy(cov, buf0.at[pl.ds(STEPS, strip)], load_sem)
    load.start()

    barrier = pltpu.get_barrier_semaphore()

    @pl.when(at_edge)
    def _():
        for peer in (
            jnp.where(lower, ncol - 4, 0),
            jnp.where(lower, ncol - 1, 3),
            jnp.where(lower, ncol - 8, 7),
        ):
            pl.semaphore_signal(barrier, inc=1, device_id=(row, peer), device_id_type=MESH)

    @pl.when(relays | pass_relay)
    def _():
        pl.semaphore_signal(barrier, inc=1, device_id=(row, relay_from), device_id_type=MESH)

    count = jnp.where(at_edge, 3, 0) + jnp.where(relays | pass_relay, 1, 0)
    for there, peer in ((has_up, up), (has_down, down), (next_left, left), (next_right, right)):

        @pl.when(there)
        def _(peer=peer):
            pl.semaphore_signal(barrier, inc=1, device_id=peer, device_id_type=MESH)

        count = count + jnp.where(there, 1, 0)

    pl.semaphore_wait(barrier, count)

    to_up = pltpu.make_async_remote_copy(
        src_ref=cov.at[pl.ds(0, STEPS)], dst_ref=buf0.at[pl.ds(strip + STEPS, STEPS)],
        send_sem=row_send.at[0], recv_sem=row_recv.at[0], device_id=up, device_id_type=MESH,
    )
    to_down = pltpu.make_async_remote_copy(
        src_ref=cov.at[pl.ds(strip - STEPS, STEPS)], dst_ref=buf0.at[pl.ds(0, STEPS)],
        send_sem=row_send.at[1], recv_sem=row_recv.at[1], device_id=down, device_id_type=MESH,
    )

    @pl.when(has_up)
    def _():
        to_up.start()

    @pl.when(has_down)
    def _():
        to_down.start()

    first_row = row * strip - STEPS

    def rows_step(src, dst, step, first, last, base):
        def one(place, carry):
            mid, east, west, north, south = weights_at(weights, index, step, first_row + place)
            for half in range(width // 128):
                lanes = pl.ds(half * 128, 128)
                value = src[place, :, lanes]
                value = (
                    mid * value
                    + east * pltpu.roll(value, nlon - 1, 0)
                    + west * pltpu.roll(value, 1, 0)
                    + north * src[place + 1, :, lanes]
                    + south * src[place - 1, :, lanes]
                )
                if step < STEPS - 1:
                    dst[place - base, :, lanes] = value
                else:
                    high = value.astype(BF16)
                    sb[place - base, :, lanes] = high
                    dst[place - base, :, lanes] = (value - high.astype(F32)).astype(BF16)
            return carry

        lax.fori_loop(first, last, one, 0)

    def first_message(i, side):
        lat = chunk_of(i)
        return pltpu.make_async_remote_copy(
            src_ref=sb.at[lat], dst_ref=(l2, r2)[side].at[lat],
            send_sem=one_send.at[side, i], recv_sem=one_recv.at[side, i],
            device_id=(right, left)[side], device_id_type=MESH,
        )

    def to_relay(i, side):
        near, away = ((3, 0), (ncol - 4, ncol - 1))[side]
        return pltpu.make_async_remote_copy(
            src_ref=sb.at[chunk_of(i)], dst_ref=held.at[i // 2],
            send_sem=one_send.at[side, i], recv_sem=held_recv.at[i // 2],
            device_id=(row, jnp.where(lax.rem(i, 2) == 0, near, away)), device_id_type=MESH,
        )

    def from_relay(j, side):
        i = 2 * j + jnp.where(near_relay, 0, 1)
        return pltpu.make_async_remote_copy(
            src_ref=held.at[j], dst_ref=(l2, r2)[side].at[chunk_of(i)],
            send_sem=held_send.at[j], recv_sem=one_recv.at[side, i],
            device_id=(row, relay_to), device_id_type=MESH,
        )

    def second_message(i, side):
        lat = chunk_of(i)
        lanes = (pl.ds(128, 128), pl.ds(0, 128))[side]
        return pltpu.make_async_remote_copy(
            src_ref=(l2, r2)[side].at[lat, :, lanes],
            dst_ref=far.at[lat, :, pl.ds(side * 128, 128)],
            send_sem=two_send.at[side, i], recv_sem=two_recv.at[side, i],
            device_id=(right, left)[side], device_id_type=MESH,
        )

    def send_first(start, stop):
        def one(i, carry):
            @pl.when(has_right & (col != edge))
            def _():
                first_message(i, 0).start()

            @pl.when(col == edge)
            def _():
                to_relay(i, 0).start()

            @pl.when(has_left & (col != edge + 1))
            def _():
                first_message(i, 1).start()

            @pl.when(col == edge + 1)
            def _():
                to_relay(i, 1).start()

            return carry

        lax.fori_loop(start, stop, one, 0)

    @pl.when(jnp.logical_not(has_up))
    def _():
        buf0[pl.ds(0, STEPS)] = jnp.zeros((STEPS, nlon, width), F32)

    @pl.when(jnp.logical_not(has_down))
    def _():
        buf0[pl.ds(strip + STEPS, STEPS)] = jnp.zeros((STEPS, nlon, width), F32)

    @pl.when(jnp.logical_not(has_left))
    def _():
        l2[...] = jnp.zeros(l2.shape, BF16)

    @pl.when(jnp.logical_not(has_right))
    def _():
        r2[...] = jnp.zeros(r2.shape, BF16)

    @pl.when(col <= 1)
    def _():
        far[:, :, 0:128] = jnp.zeros((strip, nlon, 128), BF16)

    @pl.when(col >= ncol - 2)
    def _():
        far[:, :, 128:256] = jnp.zeros((strip, nlon, 128), BF16)

    put_weights(weights, table, diffusivity)
    load.wait()
    rows_step(buf0, buf1, 0, 4, 10, 0)
    rows_step(buf1, buf2, 1, 5, 9, 0)
    rows_step(buf2, low, 2, 6, 8, STEPS)
    send_first(0, 2)

    def end_rows(bottom):
        @pl.when(jnp.logical_not(bottom) & has_up)
        def _():
            to_down.wait_recv()

        @pl.when(bottom & has_down)
        def _():
            to_up.wait_recv()

        for src, dst, step, top_first, bottom_first, base in (
            (buf0, buf1, 0, 1, strip + 2, 0),
            (buf1, buf2, 1, 2, strip + 1, 0),
            (buf2, low, 2, 3, strip, STEPS),
        ):
            first = jnp.where(bottom, bottom_first, top_first)
            rows_step(src, dst, step, first, first + STEPS, base)

    def pass_to_relay(i, side):
        lanes = (pl.ds(128, 128), pl.ds(0, 128))[side]
        return pltpu.make_async_remote_copy(
            src_ref=(l2, r2)[side].at[chunk_of(i), :, lanes], dst_ref=held_far.at[i],
            send_sem=two_send.at[side, i], recv_sem=far_recv.at[i],
            device_id=(row, (7, ncol - 8)[side]), device_id_type=MESH,
        )

    def pass_from_relay(i, side):
        return pltpu.make_async_remote_copy(
            src_ref=held_far.at[i], dst_ref=far.at[chunk_of(i), :, pl.ds(side * 128, 128)],
            send_sem=far_send.at[i], recv_sem=two_recv.at[side, i],
            device_id=(row, relay_to), device_id_type=MESH,
        )

    def pass_on(i, side, there, onward):
        @pl.when(there)
        def _():
            first_message(i, side).wait_recv()

            @pl.when(onward)
            def _():
                second_message(i, side).start()

            @pl.when(col == edge + side)
            def _():
                pass_to_relay(i, side).start()

    def columns(i):
        lat = chunk_of(i)

        @pl.when(col > 1)
        def _():
            second_message(i, 0).wait_recv()

        @pl.when(col < ncol - 2)
        def _():
            second_message(i, 1).wait_recv()

        def dot(x, w):
            return jnp.dot(x, w, preferred_element_type=F32)

        total = dot(low[lat], w_high[2])
        for place, ref in enumerate((far, l2, sb, r2)):
            x = ref[lat]
            total = total + dot(x, w_high[place]) + dot(x, w_low[place])
        ob[lat] = total
        for half in range(2):

            @pl.when(row * strip + lat == col * 2 + half)
            def _(half=half):
                lanes = pl.ds(half * 128, 128)
                own = lax.broadcasted_iota(jnp.int32, (128, 128), 0) == lax.broadcasted_iota(
                    jnp.int32, (128, 128), 1
                )
                line = noise[pl.ds(lat, 1), :]
                ob[lat, :, lanes] = ob[lat, :, lanes] + jnp.where(own, line, 0.0)

    def relay_turn(i):
        for side, here in ((0, lower), (1, jnp.logical_not(lower))):

            @pl.when(here & ((near_relay & (lax.rem(i, 2) == 0)) | (far_relay & (lax.rem(i, 2) == 1))))
            def _(side=side):
                to_relay(i, side).wait_recv()
                from_relay(i // 2, side).start()

    def relay_turns(start, stop):
        def one(i, carry):
            relay_turn(i)
            return carry

        lax.fori_loop(start, stop, one, 0)

    even = lax.rem(row, 2) == 0
    relay_turns(0, 2)
    end_rows(even)
    send_first(2, 5)
    relay_turns(2, 5)
    sub = lax.broadcasted_iota(jnp.int32, (8, 128), 0)
    middle = lax.broadcasted_iota(jnp.int32, (8, 128), 1) == 64
    v = [jnp.where((sub == n) & middle, 1.0, 0.0).astype(F32) for n in range(8)]
    for step in range(STEPS):
        fresh = []
        for n in range(1, len(v) - 1):
            mid, east, west, north, south = weights_at(weights, index, step, 2 * col - STEPS + n + step)
            fresh.append(
                mid * v[n]
                + east * pltpu.roll(v[n], 127, 1)
                + west * pltpu.roll(v[n], 1, 1)
                + north * v[n + 1]
                + south * v[n - 1]
            )
        v = fresh
    for place, lat in enumerate((0, 7, 1, 2, 3, 4, 5, 6)):
        for half in range(2):
            line = jnp.broadcast_to(v[half][lat : lat + 1, :], (128, 128))
            block = pltpu.roll(line, 64, 1, stride=1, stride_axis=0)
            rows, lanes = pl.ds((place % 2) * 128, 128), pl.ds(half * 128, 128)
            high = block.astype(BF16)
            w_high[place // 2, rows, lanes] = high
            w_low[place // 2, rows, lanes] = (block - high.astype(F32)).astype(BF16)

    def turn(i, carry):
        @pl.when((i > 1) & (i < 5))
        def _():
            relay_turn(i + 3)

        pass_on(i, 0, next_left, next_right)
        pass_on(i, 1, next_right, next_left)
        for side, here in ((0, lower), (1, jnp.logical_not(lower))):

            @pl.when(here & pass_relay & (i > 0))
            def _(side=side):
                pass_to_relay(i - 1, side).wait_recv()
                pass_from_relay(i - 1, side).start()

        return carry

    lax.fori_loop(0, 2, turn, 0)
    end_rows(jnp.logical_not(even))
    send_first(5, 8)
    lax.fori_loop(2, strip, turn, 0)
    for side, here in ((0, lower), (1, jnp.logical_not(lower))):

        @pl.when(here & pass_relay)
        def _(side=side):
            pass_to_relay(strip - 1, side).wait_recv()
            pass_from_relay(strip - 1, side).start()

    def last_turn(i, carry):
        pass_on(i, 0, col == edge + 1, True)
        pass_on(i, 1, col == edge, True)
        columns(i)
        return carry

    lax.fori_loop(0, strip, last_turn, 0)

    def finish(i, carry):
        @pl.when(has_right)
        def _():
            first_message(i, 0).wait_send()

        @pl.when(has_left)
        def _():
            first_message(i, 1).wait_send()

        @pl.when(has_left & has_right)
        def _():
            second_message(i, 0).wait_send()
            second_message(i, 1).wait_send()

        return carry

    lax.fori_loop(0, strip, finish, 0)

    @pl.when(relays)
    def _():
        for j in range(strip // 2):
            from_relay(j, 0).wait_send()

    @pl.when(pass_relay)
    def _():
        for i in range(strip):
            pass_from_relay(i, 0).wait_send()


    @pl.when(has_up)
    def _():
        to_up.wait_send()

    @pl.when(has_down)
    def _():
        to_down.wait_send()


def solution(mesh):
    nrow, ncol = mesh.shape["row"], mesh.shape["col"]

    def body(covariance, noise_var, wind_table, diffusivity, wind_index):
        rows_dev, cols_dev = covariance.shape
        strip, nlon = noise_var.shape
        nlat = wind_index.shape[1]
        block = (strip, nlon, cols_dev)
        span = (strip + 2 * STEPS, nlon, cols_dev)
        anywhere = pl.BlockSpec(memory_space=pltpu.HBM)
        scalars = pl.BlockSpec(memory_space=pltpu.SMEM)
        out, s = pl.pallas_call(
            functools.partial(kernel, nlat, nrow, ncol),
            out_shape=(jax.ShapeDtypeStruct(block, F32), jax.ShapeDtypeStruct(block, BF16)),
            in_specs=[anywhere, pl.BlockSpec(memory_space=pltpu.VMEM), scalars, scalars, scalars],
            out_specs=(pl.BlockSpec(memory_space=pltpu.VMEM),) * 2,
            scratch_shapes=[
                pltpu.VMEM(span, F32),
                pltpu.VMEM(span, F32),
                pltpu.VMEM(span, F32),
                pltpu.VMEM(block, BF16),
                pltpu.VMEM(block, BF16),
                pltpu.VMEM(block, BF16),
                pltpu.VMEM(block, BF16),
                pltpu.VMEM((strip // 2, nlon, cols_dev), BF16),
                pltpu.VMEM((strip, nlon, nlon), BF16),
                pltpu.VMEM((4, 256, 256), BF16),
                pltpu.VMEM((4, 256, 256), BF16),
                pltpu.SMEM((5 * diffusivity.shape[0],), F32),
                pltpu.SemaphoreType.DMA,
                pltpu.SemaphoreType.DMA((2,)),
                pltpu.SemaphoreType.DMA((2,)),
                pltpu.SemaphoreType.DMA((2, strip)),
                pltpu.SemaphoreType.DMA((2, strip)),
                pltpu.SemaphoreType.DMA((2, strip)),
                pltpu.SemaphoreType.DMA((2, strip)),
                pltpu.SemaphoreType.DMA((strip // 2,)),
                pltpu.SemaphoreType.DMA((strip // 2,)),
                pltpu.SemaphoreType.DMA((strip,)),
                pltpu.SemaphoreType.DMA((strip,)),
            ],
            compiler_params=pltpu.CompilerParams(collective_id=0, has_side_effects=True, vmem_limit_bytes=54755328),
        )(covariance.reshape(block), noise_var, wind_table.T, diffusivity, wind_index)
        return out.reshape(rows_dev, cols_dev), s.reshape(rows_dev, cols_dev)

    in_specs = (P("row", "col"), P("row", None), P(), P(), P())
    out_specs = (P("row", "col"), P("row", "col"))
    return jax.shard_map(body, mesh=mesh, in_specs=in_specs, out_specs=out_specs, check_vma=False)
```

```python
import functools

import jax
import jax.numpy as jnp
from jax import lax
from jax.experimental import pallas as pl
from jax.experimental.pallas import tpu as pltpu
from jax.sharding import PartitionSpec as P

MESH = pl.DeviceIdType.MESH
F32 = jnp.float32
BF16 = jnp.bfloat16
STEPS = 3


def chunk_of(i):
    even = lax.rem(lax.axis_index("row"), 2) == 0
    return jnp.where(i < 2, i + 3, jnp.where(even, jnp.where(i < 5, i + 3, i - 5), jnp.where(i < 5, i - 2, i)))


def put_weights(dst, table, diffusivity):
    for regime in range(diffusivity.shape[0]):
        zonal, merid, diffuse = table[0, regime], table[1, regime], diffusivity[regime]
        zz, mm = 0.5 * zonal * zonal, 0.5 * merid * merid
        dst[regime * 5] = 1.0 - zonal * zonal - merid * merid - 4.0 * diffuse
        dst[regime * 5 + 1] = zz - 0.5 * zonal + diffuse
        dst[regime * 5 + 2] = zz + 0.5 * zonal + diffuse
        dst[regime * 5 + 3] = mm - 0.5 * merid + diffuse
        dst[regime * 5 + 4] = mm + 0.5 * merid + diffuse


def weights_at(weights, index, step, lat):
    nlat = index.shape[1]
    inside = jnp.where((lat >= 0) & (lat < nlat), 1.0, 0.0).astype(F32)
    at = index[step, jnp.clip(lat, 0, nlat - 1)] * 5
    return [inside * weights[at + n] for n in range(5)]


def kernel(
    nlat, nrow, ncol,
    cov, noise_in, table_in, diffusivity_in, index_in,
    ob, sb,
    buf0, buf1, buf2, low, l2, r2, far, held, held_far, edge_out, edge_in, w_high, w_low, noise, table, diffusivity, index, weights,
    ready, load_sem, small_sem, row_send, row_recv, one_send, one_recv, rest_send, rest_recv, two_send, two_recv, held_send, held_recv, far_send, far_recv,
):
    strip, nlon, width = cov.shape
    row, col = lax.axis_index("row"), lax.axis_index("col")
    has_up, has_down = row > 0, row < nrow - 1
    has_left, has_right = col > 0, col < ncol - 1
    next_left, next_right = has_left & (col != ncol // 2), has_right & (col != ncol // 2 - 1)
    even = lax.rem(row, 2) == 0
    has_next = jnp.where(even, row, nrow - 1 - row) > 0
    near_row = (jnp.where(even, row + 1, row - 1), col)
    next_row = (lax.rem(jnp.where(even, row + nrow - 1, row + 1), nrow), col)
    left, right = (row, lax.rem(col + ncol - 1, ncol)), (row, lax.rem(col + 1, ncol))

    edge = ncol // 2 - 1
    near_relay = (col == 3) | (col == ncol - 4)
    far_relay = (col == 0) | (col == ncol - 1)
    pass_relay = (col == 7) | (col == ncol - 8)
    relays = near_relay | far_relay
    at_edge = (col == edge) | (col == edge + 1)
    lower = col <= edge
    relay_from = jnp.where(lower, edge, edge + 1)
    relay_to = jnp.where(lower, edge + 1, edge)

    load = pltpu.make_async_copy(cov, buf0.at[pl.ds(STEPS, strip)], load_sem)
    load.start()
    small = [
        pltpu.make_async_copy(src, dst, small_sem.at[n])
        for n, (src, dst) in enumerate(
            ((index_in, index), (table_in, table), (diffusivity_in, diffusivity), (noise_in, noise))
        )
    ]
    for copy in small:
        copy.start()

    barrier = pltpu.get_barrier_semaphore()

    @pl.when(at_edge)
    def _():
        for peer in (
            jnp.where(lower, ncol - 4, 0),
            jnp.where(lower, ncol - 1, 3),
            jnp.where(lower, ncol - 8, 7),
            jnp.where(lower, 0, ncol - 1),
        ):
            pl.semaphore_signal(barrier, inc=1, device_id=(row, peer), device_id_type=MESH)

    @pl.when(near_relay | pass_relay)
    def _():
        pl.semaphore_signal(barrier, inc=1, device_id=(row, relay_from), device_id_type=MESH)

    count = jnp.where(at_edge | far_relay, 2, 0) + jnp.where(near_relay | pass_relay, 1, 0)
    for there, peer in ((has_next, next_row), (row >= 0, near_row), (next_left, left), (next_right, right)):

        @pl.when(there)
        def _(peer=peer):
            pl.semaphore_signal(barrier, inc=1, device_id=peer, device_id_type=MESH)

        count = count + jnp.where(there, 1, 0)

    load.wait()
    edge_out[...] = buf0[pl.ds(jnp.where(even, STEPS, strip), STEPS)].astype(BF16)
    pl.semaphore_wait(barrier, count)

    @pl.when(far_relay)
    def _():
        pl.semaphore_signal(ready, inc=1, device_id=(row, relay_from), device_id_type=MESH)

    to_near = pltpu.make_async_remote_copy(
        src_ref=cov.at[pl.ds(jnp.where(even, strip - STEPS, 0), STEPS)],
        dst_ref=buf0.at[pl.ds(jnp.where(even, 0, strip + STEPS), STEPS)],
        send_sem=row_send.at[0], recv_sem=row_recv.at[0], device_id=near_row, device_id_type=MESH,
    )
    to_next = pltpu.make_async_remote_copy(
        src_ref=edge_out, dst_ref=edge_in,
        send_sem=row_send.at[1], recv_sem=row_recv.at[1], device_id=next_row, device_id_type=MESH,
    )

    @pl.when(has_next)
    def _():
        to_next.start()

    to_near.start()

    first_row = row * strip - STEPS

    def rows_step(src, dst, step, first, last, base):
        def one(place, carry):
            mid, east, west, north, south = weights_at(weights, index, step, first_row + place)
            for half in range(width // 128):
                lanes = pl.ds(half * 128, 128)
                value = src[place, :, lanes]
                value = (
                    mid * value
                    + east * pltpu.roll(value, nlon - 1, 0)
                    + west * pltpu.roll(value, 1, 0)
                    + north * src[place + 1, :, lanes]
                    + south * src[place - 1, :, lanes]
                )
                if step < STEPS - 1:
                    dst[place - base, :, lanes] = value
                else:
                    high = value.astype(BF16)
                    sb[place - base, :, lanes] = high
                    dst[place - base, :, lanes] = (value - high.astype(F32)).astype(BF16)
            return carry

        lax.fori_loop(first, last, one, 0)

    def piece(i, side, near):
        lat = chunk_of(i)
        lanes = pl.ds(128 if (side == 0) == near else 0, 128)
        send, recv = (one_send, one_recv) if near else (rest_send, rest_recv)
        return pltpu.make_async_remote_copy(
            src_ref=sb.at[lat, :, lanes], dst_ref=(l2, r2)[side].at[lat, :, lanes],
            send_sem=send.at[side, i], recv_sem=recv.at[side, i],
            device_id=(right, left)[side], device_id_type=MESH,
        )

    def first_message(i, side):
        return piece(i, side, True)

    def to_relay(i, side):
        near, away = ((3, 0), (ncol - 4, ncol - 1))[side]
        return pltpu.make_async_remote_copy(
            src_ref=sb.at[chunk_of(i)], dst_ref=held.at[i // 2],
            send_sem=one_send.at[side, i], recv_sem=held_recv.at[i // 2],
            device_id=(row, jnp.where(lax.rem(i, 2) == 0, near, away)), device_id_type=MESH,
        )

    def from_relay(j, side, i):
        return pltpu.make_async_remote_copy(
            src_ref=held.at[j], dst_ref=(l2, r2)[side].at[chunk_of(i)],
            send_sem=held_send.at[j], recv_sem=one_recv.at[side, i],
            device_id=(row, relay_to), device_id_type=MESH,
        )

    def second_message(i, side):
        lat = chunk_of(i)
        lanes = (pl.ds(128, 128), pl.ds(0, 128))[side]
        return pltpu.make_async_remote_copy(
            src_ref=(l2, r2)[side].at[lat, :, lanes],
            dst_ref=far.at[lat, :, pl.ds(side * 128, 128)],
            send_sem=two_send.at[side, i], recv_sem=two_recv.at[side, i],
            device_id=(right, left)[side], device_id_type=MESH,
        )

    def send_near(start, stop):
        def one(i, carry):
            @pl.when(next_right)
            def _():
                first_message(i, 0).start()

            @pl.when(next_left)
            def _():
                first_message(i, 1).start()

            return carry

        lax.fori_loop(start, stop, one, 0)

    def send_far(start, stop, by):
        def one(n, carry):
            i = start + n * by

            @pl.when(col == edge)
            def _():
                to_relay(i, 0).start()

            @pl.when(col == edge + 1)
            def _():
                to_relay(i, 1).start()

            return carry

        lax.fori_loop(0, (stop - start + by - 1) // by, one, 0)

    def send_rest(start, stop):
        def one(i, carry):
            @pl.when(next_right)
            def _():
                piece(i, 0, False).start()

            @pl.when(next_left)
            def _():
                piece(i, 1, False).start()

            return carry

        lax.fori_loop(start, stop, one, 0)

    @pl.when(jnp.logical_not(has_up))
    def _():
        buf0[pl.ds(0, STEPS)] = jnp.zeros((STEPS, nlon, width), F32)

    @pl.when(jnp.logical_not(has_down))
    def _():
        buf0[pl.ds(strip + STEPS, STEPS)] = jnp.zeros((STEPS, nlon, width), F32)

    @pl.when(jnp.logical_not(has_left))
    def _():
        l2[...] = jnp.zeros(l2.shape, BF16)

    @pl.when(jnp.logical_not(has_right))
    def _():
        r2[...] = jnp.zeros(r2.shape, BF16)

    @pl.when(col <= 1)
    def _():
        far[:, :, 0:128] = jnp.zeros((strip, nlon, 128), BF16)

    @pl.when(col >= ncol - 2)
    def _():
        far[:, :, 128:256] = jnp.zeros((strip, nlon, 128), BF16)

    for copy in small:
        copy.wait()
    put_weights(weights, table, diffusivity)
    rows_step(buf0, buf1, 0, 4, 10, 0)
    rows_step(buf1, buf2, 1, 5, 9, 0)
    rows_step(buf2, low, 2, 6, 8, STEPS)
    send_near(0, 2)
    send_far(0, 1, 1)
    send_rest(0, 2)

    def end_rows(bottom):
        for src, dst, step, top_first, bottom_first, base in (
            (buf0, buf1, 0, 1, strip + 2, 0),
            (buf1, buf2, 1, 2, strip + 1, 0),
            (buf2, low, 2, 3, strip, STEPS),
        ):
            first = jnp.where(bottom, bottom_first, top_first)
            rows_step(src, dst, step, first, first + STEPS, base)

    def pass_to_relay(i, side):
        lanes = (pl.ds(128, 128), pl.ds(0, 128))[side]
        return pltpu.make_async_remote_copy(
            src_ref=(l2, r2)[side].at[chunk_of(i), :, lanes], dst_ref=held_far.at[i],
            send_sem=two_send.at[side, i], recv_sem=far_recv.at[i],
            device_id=(row, (7, ncol - 8)[side]), device_id_type=MESH,
        )

    def pass_from_relay(i, side):
        return pltpu.make_async_remote_copy(
            src_ref=held_far.at[i], dst_ref=far.at[chunk_of(i), :, pl.ds(side * 128, 128)],
            send_sem=far_send.at[i], recv_sem=two_recv.at[side, i],
            device_id=(row, relay_to), device_id_type=MESH,
        )

    def pass_on(i, side, there, onward):
        @pl.when(there)
        def _():
            first_message(i, side).wait_recv()

            @pl.when(onward)
            def _():
                second_message(i, side).start()

            @pl.when(col == edge + side)
            def _():
                pass_to_relay(i, side).start()

    def columns(i):
        lat = chunk_of(i)

        @pl.when(next_left)
        def _():
            piece(i, 0, False).wait_recv()

        @pl.when(next_right)
        def _():
            piece(i, 1, False).wait_recv()

        @pl.when(col > 1)
        def _():
            second_message(i, 0).wait_recv()

        @pl.when(col < ncol - 2)
        def _():
            second_message(i, 1).wait_recv()

        def dot(x, w):
            return jnp.dot(x, w, preferred_element_type=F32)

        total = dot(low[lat], w_high[2])
        for place, ref in enumerate((far, l2, sb, r2)):
            x = ref[lat]
            total = total + dot(x, w_high[place]) + dot(x, w_low[place])
        ob[lat] = total
        for half in range(2):

            @pl.when(row * strip + lat == col * 2 + half)
            def _(half=half):
                lanes = pl.ds(half * 128, 128)
                own = lax.broadcasted_iota(jnp.int32, (128, 128), 0) == lax.broadcasted_iota(
                    jnp.int32, (128, 128), 1
                )
                line = noise[pl.ds(lat, 1), :]
                ob[lat, :, lanes] = ob[lat, :, lanes] + jnp.where(own, line, 0.0)

    def relay_turn(i):
        for side, here in ((0, lower), (1, jnp.logical_not(lower))):

            @pl.when(here & ((near_relay & (lax.rem(i, 2) == 0)) | (far_relay & (lax.rem(i, 2) == 1))))
            def _(side=side):
                to_relay(i, side).wait_recv()
                from_relay(i // 2, side, i).start()

    def relay_turns(start, stop):
        def one(i, carry):
            relay_turn(i)
            return carry

        lax.fori_loop(start, stop, one, 0)

    relay_turns(0, 1)
    to_near.wait_recv()
    end_rows(even)
    send_near(2, 5)
    send_rest(2, 4)

    @pl.when(at_edge)
    def _():
        pl.semaphore_wait(ready, 1)

    send_far(1, 5, 1)
    relay_turns(1, 3)
    sub = lax.broadcasted_iota(jnp.int32, (8, 128), 0)
    middle = lax.broadcasted_iota(jnp.int32, (8, 128), 1) == 64
    v = [jnp.where((sub == n) & middle, 1.0, 0.0).astype(F32) for n in range(8)]
    for step in range(STEPS):
        fresh = []
        for n in range(1, len(v) - 1):
            mid, east, west, north, south = weights_at(weights, index, step, 2 * col - STEPS + n + step)
            fresh.append(
                mid * v[n]
                + east * pltpu.roll(v[n], 127, 1)
                + west * pltpu.roll(v[n], 1, 1)
                + north * v[n + 1]
                + south * v[n - 1]
            )
        v = fresh
    for place, lat in enumerate((0, 7, 1, 2, 3, 4, 5, 6)):
        for half in range(2):
            line = jnp.broadcast_to(v[half][lat : lat + 1, :], (128, 128))
            block = pltpu.roll(line, 64, 1, stride=1, stride_axis=0)
            rows, lanes = pl.ds((place % 2) * 128, 128), pl.ds(half * 128, 128)
            high = block.astype(BF16)
            w_high[place // 2, rows, lanes] = high
            w_low[place // 2, rows, lanes] = (block - high.astype(F32)).astype(BF16)

    def turn(i, carry):
        @pl.when((i > 1) & (i < 5))
        def _():
            relay_turn(i + 3)

        @pl.when(pass_relay & jnp.logical_not(lower))
        def _():
            def one(n, carry):
                pass_to_relay(n, 1).wait_recv()
                pass_from_relay(n, 1).start()
                return carry

            lax.fori_loop(i + jnp.where(i > 2, 1, 0), jnp.minimum(i + jnp.where(i > 1, 2, 1), strip), one, 0)

        pass_on(i, 0, next_left, next_right)
        pass_on(i, 1, next_right, next_left)
        @pl.when(pass_relay & lower & (i > 0))
        def _():
            pass_to_relay(i - 1, 0).wait_recv()
            pass_from_relay(i - 1, 0).start()

        return carry

    lax.fori_loop(0, 2, turn, 0)

    @pl.when(has_next)
    def _():
        to_next.wait_recv()
        buf0[pl.ds(jnp.where(even, 0, strip + STEPS), STEPS)] = edge_in[...].astype(F32)

    end_rows(jnp.logical_not(even))
    send_near(5, 8)
    send_far(5, 8, 1)
    send_rest(4, 8)
    relay_turns(3, 5)
    lax.fori_loop(2, strip, turn, 0)
    @pl.when(pass_relay & lower)
    def _():
        pass_to_relay(strip - 1, 0).wait_recv()
        pass_from_relay(strip - 1, 0).start()

    def edge_turn(i, carry):
        @pl.when(col == edge + 1)
        def _():
            from_relay(i // 2, 0, i).wait_recv()
            second_message(i, 0).start()

        @pl.when(col == edge)
        def _():
            from_relay(i // 2, 1, i).wait_recv()
            second_message(i, 1).start()

        return carry

    @pl.when(at_edge)
    def _():
        lax.fori_loop(0, strip, edge_turn, 0)

    def last_turn(i, carry):
        columns(i)
        return carry

    lax.fori_loop(0, strip, last_turn, 0)

    def finish(i, carry):
        @pl.when(next_right)
        def _():
            first_message(i, 0).wait_send()
            piece(i, 0, False).wait_send()

        @pl.when(next_left)
        def _():
            first_message(i, 1).wait_send()
            piece(i, 1, False).wait_send()

        @pl.when(at_edge)
        def _():
            @pl.when(lower)
            def _():
                to_relay(i, 0).wait_send()

            @pl.when(jnp.logical_not(lower))
            def _():
                to_relay(i, 1).wait_send()

        @pl.when(has_left & has_right)
        def _():
            second_message(i, 0).wait_send()
            second_message(i, 1).wait_send()

        return carry

    lax.fori_loop(0, strip, finish, 0)

    @pl.when(relays)
    def _():
        for j in range(strip // 2):
            from_relay(j, 0, 2 * j).wait_send()

    @pl.when(pass_relay)
    def _():
        for i in range(strip):
            pass_from_relay(i, 0).wait_send()


    to_near.wait_send()

    @pl.when(has_next)
    def _():
        to_next.wait_send()


def write_out(out_in, s_in, out, s, sem):
    copies = []
    for lat in range(out.shape[0]):
        copies.append(pltpu.make_async_copy(out_in.at[lat], out.at[lat], sem.at[0, lat]))
        copies.append(pltpu.make_async_copy(s_in.at[lat], s.at[lat], sem.at[1, lat]))
    for copy in copies:
        copy.start()
    for copy in copies:
        copy.wait()


def solution(mesh):
    nrow, ncol = mesh.shape["row"], mesh.shape["col"]

    def body(covariance, noise_var, wind_table, diffusivity, wind_index):
        rows_dev, cols_dev = covariance.shape
        strip, nlon = noise_var.shape
        nlat = wind_index.shape[1]
        block = (strip, nlon, cols_dev)
        span = (strip + 2 * STEPS, nlon, cols_dev)
        anywhere = pl.BlockSpec(memory_space=pltpu.HBM)
        held_out, held_s = pl.pallas_call(
            functools.partial(kernel, nlat, nrow, ncol),
            out_shape=(jax.ShapeDtypeStruct(block, F32), jax.ShapeDtypeStruct(block, BF16)),
            in_specs=[anywhere] * 5,
            out_specs=(pl.BlockSpec(memory_space=pltpu.VMEM),) * 2,
            scratch_shapes=[
                pltpu.VMEM(span, F32),
                pltpu.VMEM(span, F32),
                pltpu.VMEM(span, F32),
                pltpu.VMEM(block, BF16),
                pltpu.VMEM(block, BF16),
                pltpu.VMEM(block, BF16),
                pltpu.VMEM(block, BF16),
                pltpu.VMEM((strip // 2, nlon, cols_dev), BF16),
                pltpu.VMEM((strip, nlon, nlon), BF16),
                pltpu.VMEM((STEPS, nlon, cols_dev), BF16),
                pltpu.VMEM((STEPS, nlon, cols_dev), BF16),
                pltpu.VMEM((4, 256, 256), BF16),
                pltpu.VMEM((4, 256, 256), BF16),
                pltpu.VMEM(noise_var.shape, F32),
                pltpu.SMEM(wind_table.shape[::-1], F32),
                pltpu.SMEM(diffusivity.shape, F32),
                pltpu.SMEM(wind_index.shape, jnp.int32),
                pltpu.SMEM((5 * diffusivity.shape[0],), F32),
                pltpu.SemaphoreType.REGULAR,
                pltpu.SemaphoreType.DMA,
                pltpu.SemaphoreType.DMA((4,)),
                pltpu.SemaphoreType.DMA((2,)),
                pltpu.SemaphoreType.DMA((2,)),
                pltpu.SemaphoreType.DMA((2, strip)),
                pltpu.SemaphoreType.DMA((2, strip)),
                pltpu.SemaphoreType.DMA((2, strip)),
                pltpu.SemaphoreType.DMA((2, strip)),
                pltpu.SemaphoreType.DMA((2, strip)),
                pltpu.SemaphoreType.DMA((2, strip)),
                pltpu.SemaphoreType.DMA((strip // 2,)),
                pltpu.SemaphoreType.DMA((strip // 2,)),
                pltpu.SemaphoreType.DMA((strip,)),
                pltpu.SemaphoreType.DMA((strip,)),
            ],
            compiler_params=pltpu.CompilerParams(collective_id=0, has_side_effects=True, vmem_limit_bytes=54755328),
        )(*(
            pltpu.with_memory_space_constraint(x, pltpu.HBM)
            for x in (covariance.reshape(block), noise_var, wind_table.T, diffusivity, wind_index)
        ))
        out, s = pl.pallas_call(
            write_out,
            out_shape=(jax.ShapeDtypeStruct(block, F32), jax.ShapeDtypeStruct(block, BF16)),
            in_specs=[pl.BlockSpec(memory_space=pltpu.VMEM)] * 2,
            out_specs=(anywhere, anywhere),
            scratch_shapes=[pltpu.SemaphoreType.DMA((2, strip))],
            compiler_params=pltpu.CompilerParams(vmem_limit_bytes=1 << 20),
        )(held_out, held_s)
        return out.reshape(rows_dev, cols_dev), s.reshape(rows_dev, cols_dev)

    in_specs = (P("row", "col"), P("row", None), P(), P(), P())
    out_specs = (P("row", "col"), P("row", "col"))
    return jax.shard_map(body, mesh=mesh, in_specs=in_specs, out_specs=out_specs, check_vma=False)
```

```python
import functools

import jax
import jax.numpy as jnp
from jax import lax
from jax.experimental import pallas as pl
from jax.experimental.pallas import tpu as pltpu
from jax.sharding import PartitionSpec as P

MESH = pl.DeviceIdType.MESH
F32 = jnp.float32
BF16 = jnp.bfloat16
STEPS = 3
LAG = 3


def chunk_of(i):
    even = lax.rem(lax.axis_index("row"), 2) == 0
    return jnp.where(i < 2, i + 3, jnp.where(even, jnp.where(i < 5, i + 3, i - 5), jnp.where(i < 5, i - 2, i)))


def put_weights(dst, table, diffusivity):
    for regime in range(diffusivity.shape[0]):
        zonal, merid, diffuse = table[0, regime], table[1, regime], diffusivity[regime]
        zz, mm = 0.5 * zonal * zonal, 0.5 * merid * merid
        dst[regime * 5] = 1.0 - zonal * zonal - merid * merid - 4.0 * diffuse
        dst[regime * 5 + 1] = zz - 0.5 * zonal + diffuse
        dst[regime * 5 + 2] = zz + 0.5 * zonal + diffuse
        dst[regime * 5 + 3] = mm - 0.5 * merid + diffuse
        dst[regime * 5 + 4] = mm + 0.5 * merid + diffuse


def weights_at(weights, index, step, lat):
    nlat = index.shape[1]
    inside = jnp.where((lat >= 0) & (lat < nlat), 1.0, 0.0).astype(F32)
    at = index[step, jnp.clip(lat, 0, nlat - 1)] * 5
    return [inside * weights[at + n] for n in range(5)]


def kernel(
    nlat, nrow, ncol,
    cov, noise_in, table_in, diffusivity_in, index_in,
    ob, sb,
    buf0, buf1, buf2, low, l2, r2, far, held, held_far, edge_out, edge_in, w_high, w_low, noise, table, diffusivity, index, weights,
    ready, load_sem, small_sem, row_send, row_recv, one_send, one_recv, rest_recv, two_send, held_send, held_recv, far_send, far_recv,
):
    strip, nlon, width = cov.shape
    row, col = lax.axis_index("row"), lax.axis_index("col")
    has_up, has_down = row > 0, row < nrow - 1
    has_left, has_right = col > 0, col < ncol - 1
    next_left, next_right = has_left & (col != ncol // 2), has_right & (col != ncol // 2 - 1)
    even = lax.rem(row, 2) == 0
    has_next = jnp.where(even, row, nrow - 1 - row) > 0
    near_row = (jnp.where(even, row + 1, row - 1), col)
    next_row = (lax.rem(jnp.where(even, row + nrow - 1, row + 1), nrow), col)
    left, right = (row, lax.rem(col + ncol - 1, ncol)), (row, lax.rem(col + 1, ncol))

    edge = ncol // 2 - 1
    near_relay = (col == 3) | (col == ncol - 4)
    far_relay = (col == 0) | (col == ncol - 1)
    pass_relay = (col == 7) | (col == ncol - 8)
    relays = near_relay | far_relay
    at_edge = (col == edge) | (col == edge + 1)
    lower = col <= edge
    relay_from = jnp.where(lower, edge, edge + 1)
    relay_to = jnp.where(lower, edge + 1, edge)

    load = pltpu.make_async_copy(cov, buf0.at[pl.ds(STEPS, strip)], load_sem)
    load.start()
    small = [
        pltpu.make_async_copy(src, dst, small_sem.at[n])
        for n, (src, dst) in enumerate(
            ((index_in, index), (table_in, table), (diffusivity_in, diffusivity), (noise_in, noise))
        )
    ]
    for copy in small:
        copy.start()

    barrier = pltpu.get_barrier_semaphore()

    @pl.when(at_edge)
    def _():
        for peer in (
            jnp.where(lower, ncol - 4, 0),
            jnp.where(lower, ncol - 1, 3),
            jnp.where(lower, ncol - 8, 7),
            jnp.where(lower, 0, ncol - 1),
        ):
            pl.semaphore_signal(barrier, inc=1, device_id=(row, peer), device_id_type=MESH)

    @pl.when(near_relay | pass_relay)
    def _():
        pl.semaphore_signal(barrier, inc=1, device_id=(row, relay_from), device_id_type=MESH)

    count = jnp.where(at_edge | far_relay, 2, 0) + jnp.where(near_relay | pass_relay, 1, 0)
    for there, peer in ((has_next, next_row), (row >= 0, near_row), (next_left, left), (next_right, right)):

        @pl.when(there)
        def _(peer=peer):
            pl.semaphore_signal(barrier, inc=1, device_id=peer, device_id_type=MESH)

        count = count + jnp.where(there, 1, 0)

    load.wait()
    edge_out[...] = buf0[pl.ds(jnp.where(even, STEPS, strip), STEPS)].astype(BF16)
    pl.semaphore_wait(barrier, count)

    @pl.when(far_relay)
    def _():
        pl.semaphore_signal(ready, inc=1, device_id=(row, relay_from), device_id_type=MESH)

    to_near = pltpu.make_async_remote_copy(
        src_ref=cov.at[pl.ds(jnp.where(even, strip - STEPS, 0), STEPS)],
        dst_ref=buf0.at[pl.ds(jnp.where(even, 0, strip + STEPS), STEPS)],
        send_sem=row_send.at[0], recv_sem=row_recv.at[0], device_id=near_row, device_id_type=MESH,
    )
    to_next = pltpu.make_async_remote_copy(
        src_ref=edge_out, dst_ref=edge_in,
        send_sem=row_send.at[1], recv_sem=row_recv.at[1], device_id=next_row, device_id_type=MESH,
    )

    @pl.when(has_next)
    def _():
        to_next.start()

    to_near.start()

    first_row = row * strip - STEPS

    def rows_step(src, dst, step, first, last, base):
        def one(place, carry):
            mid, east, west, north, south = weights_at(weights, index, step, first_row + place)
            for half in range(width // 128):
                lanes = pl.ds(half * 128, 128)
                value = src[place, :, lanes]
                value = (
                    mid * value
                    + east * pltpu.roll(value, nlon - 1, 0)
                    + west * pltpu.roll(value, 1, 0)
                    + north * src[place + 1, :, lanes]
                    + south * src[place - 1, :, lanes]
                )
                if step < STEPS - 1:
                    dst[place - base, :, lanes] = value
                else:
                    high = value.astype(BF16)
                    sb[place - base, :, lanes] = high
                    dst[place - base, :, lanes] = (value - high.astype(F32)).astype(BF16)
            return carry

        lax.fori_loop(first, last, one, 0)

    def piece(i, side, near):
        lat = chunk_of(i)
        lanes = pl.ds(128 if (side == 0) == near else 0, 128)
        recv = one_recv if near else rest_recv
        return pltpu.make_async_remote_copy(
            src_ref=sb.at[lat, :, lanes], dst_ref=(l2, r2)[side].at[lat, :, lanes],
            send_sem=one_send.at[side], recv_sem=recv.at[side, i],
            device_id=(right, left)[side], device_id_type=MESH,
        )

    def first_message(i, side):
        return piece(i, side, True)

    def to_relay(i, side):
        near, away = ((3, 0), (ncol - 4, ncol - 1))[side]
        return pltpu.make_async_remote_copy(
            src_ref=sb.at[chunk_of(i)], dst_ref=held.at[i // 2],
            send_sem=one_send.at[side], recv_sem=held_recv.at[i // 2],
            device_id=(row, jnp.where(lax.rem(i, 2) == 0, near, away)), device_id_type=MESH,
        )

    def from_relay(j, side, i):
        return pltpu.make_async_remote_copy(
            src_ref=held.at[j], dst_ref=(l2, r2)[side].at[chunk_of(i)],
            send_sem=held_send, recv_sem=one_recv.at[side, i],
            device_id=(row, relay_to), device_id_type=MESH,
        )

    def second_message(i, side):
        lat = chunk_of(i)
        lanes = (pl.ds(128, 128), pl.ds(0, 128))[side]
        return pltpu.make_async_remote_copy(
            src_ref=(l2, r2)[side].at[lat, :, lanes],
            dst_ref=far.at[lat, :, pl.ds(side * 128, 128)],
            send_sem=two_send.at[side], recv_sem=rest_recv.at[side, i],
            device_id=(right, left)[side], device_id_type=MESH,
        )

    def send_near(start, stop):
        def one(i, carry):
            @pl.when(next_right)
            def _():
                first_message(i, 0).start()

            @pl.when(next_left)
            def _():
                first_message(i, 1).start()

            return carry

        lax.fori_loop(start, stop, one, 0)

    def send_far(start, stop, by):
        def one(n, carry):
            i = start + n * by

            @pl.when(col == edge)
            def _():
                to_relay(i, 0).start()

            @pl.when(col == edge + 1)
            def _():
                to_relay(i, 1).start()

            return carry

        lax.fori_loop(0, (stop - start + by - 1) // by, one, 0)

    def send_rest(start, stop):
        def one(i, carry):
            @pl.when(next_right)
            def _():
                piece(i, 0, False).start()

            @pl.when(next_left)
            def _():
                piece(i, 1, False).start()

            return carry

        lax.fori_loop(start, stop, one, 0)

    @pl.when(jnp.logical_not(has_up))
    def _():
        buf0[pl.ds(0, STEPS)] = jnp.zeros((STEPS, nlon, width), F32)

    @pl.when(jnp.logical_not(has_down))
    def _():
        buf0[pl.ds(strip + STEPS, STEPS)] = jnp.zeros((STEPS, nlon, width), F32)

    @pl.when(jnp.logical_not(has_left))
    def _():
        l2[...] = jnp.zeros(l2.shape, BF16)

    @pl.when(jnp.logical_not(has_right))
    def _():
        r2[...] = jnp.zeros(r2.shape, BF16)

    @pl.when(col <= 1)
    def _():
        far[:, :, 0:128] = jnp.zeros((strip, nlon, 128), BF16)

    @pl.when(col >= ncol - 2)
    def _():
        far[:, :, 128:256] = jnp.zeros((strip, nlon, 128), BF16)

    for copy in small:
        copy.wait()
    put_weights(weights, table, diffusivity)
    rows_step(buf0, buf1, 0, 4, 10, 0)
    rows_step(buf1, buf2, 1, 5, 9, 0)
    rows_step(buf2, low, 2, 6, 8, STEPS)
    send_near(0, 2)
    send_far(0, 1, 1)
    send_rest(0, 2)

    def end_rows(bottom):
        for src, dst, step, top_first, bottom_first, base in (
            (buf0, buf1, 0, 1, strip + 2, 0),
            (buf1, buf2, 1, 2, strip + 1, 0),
            (buf2, low, 2, 3, strip, STEPS),
        ):
            first = jnp.where(bottom, bottom_first, top_first)
            rows_step(src, dst, step, first, first + STEPS, base)

    def pass_to_relay(i, side):
        lanes = (pl.ds(128, 128), pl.ds(0, 128))[side]
        return pltpu.make_async_remote_copy(
            src_ref=(l2, r2)[side].at[chunk_of(i), :, lanes], dst_ref=held_far.at[i],
            send_sem=two_send.at[side], recv_sem=far_recv.at[i],
            device_id=(row, (7, ncol - 8)[side]), device_id_type=MESH,
        )

    def pass_from_relay(i, side):
        return pltpu.make_async_remote_copy(
            src_ref=held_far.at[i], dst_ref=far.at[chunk_of(i), :, pl.ds(side * 128, 128)],
            send_sem=far_send, recv_sem=rest_recv.at[side, i],
            device_id=(row, relay_to), device_id_type=MESH,
        )

    def pass_on(i, side, there, onward):
        @pl.when(there)
        def _():
            first_message(i, side).wait_recv()

            @pl.when(onward)
            def _():
                second_message(i, side).start()

            @pl.when(col == edge + side)
            def _():
                pass_to_relay(i, side).start()

    def arrival(like, recv):
        return pltpu.make_async_remote_copy(
            src_ref=like, dst_ref=like, send_sem=held_send, recv_sem=recv,
            device_id=right, device_id_type=MESH,
        )

    def departure(like, send):
        return pltpu.make_async_remote_copy(
            src_ref=like, dst_ref=like, send_sem=send, recv_sem=far_recv.at[0],
            device_id=right, device_id_type=MESH,
        )

    def columns(i):
        lat = chunk_of(i)

        for side, rest, passed in ((0, next_left, col > 1), (1, next_right, col < ncol - 2)):

            @pl.when(rest & passed)
            def _(side=side):
                arrival(sb.at[lat], rest_recv.at[side, i]).wait_recv()

            @pl.when(rest & jnp.logical_not(passed))
            def _(side=side):
                piece(i, side, False).wait_recv()

            @pl.when(passed & jnp.logical_not(rest))
            def _(side=side):
                second_message(i, side).wait_recv()

        def dot(x, w):
            return jnp.dot(x, w, preferred_element_type=F32)

        total = dot(low[lat], w_high[2])
        for place, ref in enumerate((far, l2, sb, r2)):
            x = ref[lat]
            total = total + dot(x, w_high[place]) + dot(x, w_low[place])
        ob[lat] = total
        for half in range(2):

            @pl.when(row * strip + lat == col * 2 + half)
            def _(half=half):
                lanes = pl.ds(half * 128, 128)
                own = lax.broadcasted_iota(jnp.int32, (128, 128), 0) == lax.broadcasted_iota(
                    jnp.int32, (128, 128), 1
                )
                line = noise[pl.ds(lat, 1), :]
                ob[lat, :, lanes] = ob[lat, :, lanes] + jnp.where(own, line, 0.0)

    def relay_turn(i):
        for side, here in ((0, lower), (1, jnp.logical_not(lower))):

            @pl.when(here & ((near_relay & (lax.rem(i, 2) == 0)) | (far_relay & (lax.rem(i, 2) == 1))))
            def _(side=side):
                to_relay(i, side).wait_recv()
                from_relay(i // 2, side, i).start()

    def relay_turns(start, stop):
        def one(i, carry):
            relay_turn(i)
            return carry

        lax.fori_loop(start, stop, one, 0)

    relay_turns(0, 1)
    to_near.wait_recv()
    end_rows(even)
    send_near(2, 5)
    send_rest(2, 4)

    @pl.when(at_edge)
    def _():
        pl.semaphore_wait(ready, 1)

    send_far(1, 5, 1)
    relay_turns(1, 3)
    sub = lax.broadcasted_iota(jnp.int32, (8, 128), 0)
    middle = lax.broadcasted_iota(jnp.int32, (8, 128), 1) == 64
    v = [jnp.where((sub == n) & middle, 1.0, 0.0).astype(F32) for n in range(8)]
    for step in range(STEPS):
        fresh = []
        for n in range(1, len(v) - 1):
            mid, east, west, north, south = weights_at(weights, index, step, 2 * col - STEPS + n + step)
            fresh.append(
                mid * v[n]
                + east * pltpu.roll(v[n], 127, 1)
                + west * pltpu.roll(v[n], 1, 1)
                + north * v[n + 1]
                + south * v[n - 1]
            )
        v = fresh
    for place, lat in enumerate((0, 7, 1, 2, 3, 4, 5, 6)):
        for half in range(2):
            line = jnp.broadcast_to(v[half][lat : lat + 1, :], (128, 128))
            block = pltpu.roll(line, 64, 1, stride=1, stride_axis=0)
            rows, lanes = pl.ds((place % 2) * 128, 128), pl.ds(half * 128, 128)
            high = block.astype(BF16)
            w_high[place // 2, rows, lanes] = high
            w_low[place // 2, rows, lanes] = (block - high.astype(F32)).astype(BF16)

    def turn(i, carry):
        @pl.when((i > 1) & (i < 5))
        def _():
            relay_turn(i + 3)

        @pl.when(pass_relay & jnp.logical_not(lower))
        def _():
            def one(n, carry):
                pass_to_relay(n, 1).wait_recv()
                pass_from_relay(n, 1).start()
                return carry

            lax.fori_loop(i + jnp.where(i > 2, 1, 0), jnp.minimum(i + jnp.where(i > 1, 2, 1), strip), one, 0)

        pass_on(i, 0, next_left, next_right)
        pass_on(i, 1, next_right, next_left)
        @pl.when(pass_relay & lower & (i > 0))
        def _():
            pass_to_relay(i - 1, 0).wait_recv()
            pass_from_relay(i - 1, 0).start()

        return carry

    lax.fori_loop(0, 2, turn, 0)

    @pl.when(has_next)
    def _():
        to_next.wait_recv()
        buf0[pl.ds(jnp.where(even, 0, strip + STEPS), STEPS)] = edge_in[...].astype(F32)

    end_rows(jnp.logical_not(even))
    send_near(5, 8)
    send_far(5, 8, 1)
    send_rest(4, 8)
    relay_turns(3, 5)
    lax.fori_loop(2, strip, turn, 0)
    @pl.when(pass_relay & lower)
    def _():
        pass_to_relay(strip - 1, 0).wait_recv()
        pass_from_relay(strip - 1, 0).start()

    def edge_turn(i, carry):
        @pl.when(col == edge + 1)
        def _():
            from_relay(i // 2, 0, i).wait_recv()
            second_message(i, 0).start()

        @pl.when(col == edge)
        def _():
            from_relay(i // 2, 1, i).wait_recv()
            second_message(i, 1).start()

        return carry

    def last_turn(i, carry):
        @pl.when(i < strip)
        def _():
            edge_turn(i, 0)

        @pl.when(i >= LAG)
        def _():
            columns(i - LAG)

        return carry

    lax.fori_loop(0, strip + LAG, last_turn, 0)

    for side, there in ((0, has_right), (1, has_left)):

        @pl.when(there)
        def _(side=side):
            departure(sb, one_send.at[side]).wait_send()

        @pl.when(has_left & has_right)
        def _(side=side):
            departure(held_far, two_send.at[side]).wait_send()

    @pl.when(relays)
    def _():
        departure(held, held_send).wait_send()

    @pl.when(pass_relay)
    def _():
        departure(held_far, far_send).wait_send()

    to_near.wait_send()

    @pl.when(has_next)
    def _():
        to_next.wait_send()


def write_out(out_in, s_in, out, s, sem):
    copies = []
    for lat in range(out.shape[0]):
        copies.append(pltpu.make_async_copy(out_in.at[lat], out.at[lat], sem.at[0, lat]))
        copies.append(pltpu.make_async_copy(s_in.at[lat], s.at[lat], sem.at[1, lat]))
    for copy in copies:
        copy.start()
    for copy in copies:
        copy.wait()


def solution(mesh):
    nrow, ncol = mesh.shape["row"], mesh.shape["col"]

    def body(covariance, noise_var, wind_table, diffusivity, wind_index):
        rows_dev, cols_dev = covariance.shape
        strip, nlon = noise_var.shape
        nlat = wind_index.shape[1]
        block = (strip, nlon, cols_dev)
        span = (strip + 2 * STEPS, nlon, cols_dev)
        anywhere = pl.BlockSpec(memory_space=pltpu.HBM)
        held_out, held_s = pl.pallas_call(
            functools.partial(kernel, nlat, nrow, ncol),
            out_shape=(jax.ShapeDtypeStruct(block, F32), jax.ShapeDtypeStruct(block, BF16)),
            in_specs=[anywhere] * 5,
            out_specs=(pl.BlockSpec(memory_space=pltpu.VMEM),) * 2,
            scratch_shapes=[
                pltpu.VMEM(span, F32),
                pltpu.VMEM(span, F32),
                pltpu.VMEM(span, F32),
                pltpu.VMEM(block, BF16),
                pltpu.VMEM(block, BF16),
                pltpu.VMEM(block, BF16),
                pltpu.VMEM(block, BF16),
                pltpu.VMEM((strip // 2, nlon, cols_dev), BF16),
                pltpu.VMEM((strip, nlon, nlon), BF16),
                pltpu.VMEM((STEPS, nlon, cols_dev), BF16),
                pltpu.VMEM((STEPS, nlon, cols_dev), BF16),
                pltpu.VMEM((4, 256, 256), BF16),
                pltpu.VMEM((4, 256, 256), BF16),
                pltpu.VMEM(noise_var.shape, F32),
                pltpu.SMEM(wind_table.shape[::-1], F32),
                pltpu.SMEM(diffusivity.shape, F32),
                pltpu.SMEM(wind_index.shape, jnp.int32),
                pltpu.SMEM((5 * diffusivity.shape[0],), F32),
                pltpu.SemaphoreType.REGULAR,
                pltpu.SemaphoreType.DMA,
                pltpu.SemaphoreType.DMA((4,)),
                pltpu.SemaphoreType.DMA((2,)),
                pltpu.SemaphoreType.DMA((2,)),
                pltpu.SemaphoreType.DMA((2,)),
                pltpu.SemaphoreType.DMA((2, strip)),
                pltpu.SemaphoreType.DMA((2, strip)),
                pltpu.SemaphoreType.DMA((2,)),
                pltpu.SemaphoreType.DMA,
                pltpu.SemaphoreType.DMA((strip // 2,)),
                pltpu.SemaphoreType.DMA,
                pltpu.SemaphoreType.DMA((strip,)),
            ],
            compiler_params=pltpu.CompilerParams(collective_id=0, has_side_effects=True, vmem_limit_bytes=54755328),
        )(*(
            pltpu.with_memory_space_constraint(x, pltpu.HBM)
            for x in (covariance.reshape(block), noise_var, wind_table.T, diffusivity, wind_index)
        ))
        out, s = pl.pallas_call(
            write_out,
            out_shape=(jax.ShapeDtypeStruct(block, F32), jax.ShapeDtypeStruct(block, BF16)),
            in_specs=[pl.BlockSpec(memory_space=pltpu.VMEM)] * 2,
            out_specs=(anywhere, anywhere),
            scratch_shapes=[pltpu.SemaphoreType.DMA((2, strip))],
            compiler_params=pltpu.CompilerParams(vmem_limit_bytes=1 << 20),
        )(held_out, held_s)
        return out.reshape(rows_dev, cols_dev), s.reshape(rows_dev, cols_dev)

    in_specs = (P("row", "col"), P("row", None), P(), P(), P())
    out_specs = (P("row", "col"), P("row", "col"))
    return jax.shard_map(body, mesh=mesh, in_specs=in_specs, out_specs=out_specs, check_vma=False)
```

```python
import functools

import jax
import jax.numpy as jnp
from jax import lax
from jax.experimental import pallas as pl
from jax.experimental.pallas import tpu as pltpu
from jax.sharding import PartitionSpec as P

MESH = pl.DeviceIdType.MESH
F32 = jnp.float32
BF16 = jnp.bfloat16
STEPS = 3
LAG = 3
JOINT = 5


def chunk_of(i):
    even = lax.rem(lax.axis_index("row"), 2) == 0
    return jnp.where(i < 2, i + 3, jnp.where(even, jnp.where(i < 5, i + 3, i - 5), jnp.where(i < 5, i - 2, i)))


def put_weights(dst, table, diffusivity):
    for regime in range(diffusivity.shape[0]):
        zonal, merid, diffuse = table[0, regime], table[1, regime], diffusivity[regime]
        zz, mm = 0.5 * zonal * zonal, 0.5 * merid * merid
        dst[regime * 5] = 1.0 - zonal * zonal - merid * merid - 4.0 * diffuse
        dst[regime * 5 + 1] = zz - 0.5 * zonal + diffuse
        dst[regime * 5 + 2] = zz + 0.5 * zonal + diffuse
        dst[regime * 5 + 3] = mm - 0.5 * merid + diffuse
        dst[regime * 5 + 4] = mm + 0.5 * merid + diffuse


def weights_at(weights, index, step, lat):
    nlat = index.shape[1]
    inside = jnp.where((lat >= 0) & (lat < nlat), 1.0, 0.0).astype(F32)
    at = index[step, jnp.clip(lat, 0, nlat - 1)] * 5
    return [inside * weights[at + n] for n in range(5)]


def kernel(
    nlat, nrow, ncol,
    cov, noise_in, table_in, diffusivity_in, index_in,
    ob, sb,
    buf0, buf1, buf2, low, l2, r2, far, held, held_far, edge_out, edge_in, w_high, w_low, noise, table, diffusivity, index, weights,
    ready, load_sem, small_sem, row_send, row_recv, one_send, one_recv, rest_recv, two_send, two_recv, held_send, held_recv, far_send, far_recv,
):
    strip, nlon, width = cov.shape
    row, col = lax.axis_index("row"), lax.axis_index("col")
    has_up, has_down = row > 0, row < nrow - 1
    has_left, has_right = col > 0, col < ncol - 1
    next_left, next_right = has_left & (col != ncol // 2), has_right & (col != ncol // 2 - 1)
    even = lax.rem(row, 2) == 0
    has_next = jnp.where(even, row, nrow - 1 - row) > 0
    near_row = (jnp.where(even, row + 1, row - 1), col)
    next_row = (lax.rem(jnp.where(even, row + nrow - 1, row + 1), nrow), col)
    left, right = (row, lax.rem(col + ncol - 1, ncol)), (row, lax.rem(col + 1, ncol))

    edge = ncol // 2 - 1
    near_relay = (col == 3) | (col == ncol - 4)
    far_relay = (col == 0) | (col == ncol - 1)
    pass_relay = (col == 7) | (col == ncol - 8)
    relays = near_relay | far_relay
    at_edge = (col == edge) | (col == edge + 1)
    lower = col <= edge
    relay_from = jnp.where(lower, edge, edge + 1)
    relay_to = jnp.where(lower, edge + 1, edge)

    load = pltpu.make_async_copy(cov, buf0.at[pl.ds(STEPS, strip)], load_sem)
    load.start()
    small = [
        pltpu.make_async_copy(src, dst, small_sem.at[n])
        for n, (src, dst) in enumerate(
            ((index_in, index), (table_in, table), (diffusivity_in, diffusivity), (noise_in, noise))
        )
    ]
    for copy in small:
        copy.start()

    barrier = pltpu.get_barrier_semaphore()

    @pl.when(at_edge)
    def _():
        for peer in (
            jnp.where(lower, ncol - 4, 0),
            jnp.where(lower, ncol - 1, 3),
            jnp.where(lower, ncol - 8, 7),
            jnp.where(lower, 0, ncol - 1),
        ):
            pl.semaphore_signal(barrier, inc=1, device_id=(row, peer), device_id_type=MESH)

    @pl.when(near_relay | pass_relay)
    def _():
        pl.semaphore_signal(barrier, inc=1, device_id=(row, relay_from), device_id_type=MESH)

    count = jnp.where(at_edge | far_relay, 2, 0) + jnp.where(near_relay | pass_relay, 1, 0)
    for there, peer in ((has_next, next_row), (row >= 0, near_row), (next_left, left), (next_right, right)):

        @pl.when(there)
        def _(peer=peer):
            pl.semaphore_signal(barrier, inc=1, device_id=peer, device_id_type=MESH)

        count = count + jnp.where(there, 1, 0)

    load.wait()
    edge_out[...] = buf0[pl.ds(jnp.where(even, STEPS, strip), STEPS)].astype(BF16)
    first_row = row * strip - STEPS

    def rows_step(src, dst, step, first, last, base):
        def one(place, carry):
            mid, east, west, north, south = weights_at(weights, index, step, first_row + place)
            for half in range(width // 128):
                lanes = pl.ds(half * 128, 128)
                value = src[place, :, lanes]
                value = (
                    mid * value
                    + east * pltpu.roll(value, nlon - 1, 0)
                    + west * pltpu.roll(value, 1, 0)
                    + north * src[place + 1, :, lanes]
                    + south * src[place - 1, :, lanes]
                )
                if step < STEPS - 1:
                    dst[place - base, :, lanes] = value
                else:
                    high = value.astype(BF16)
                    sb[place - base, :, lanes] = high
                    dst[place - base, :, lanes] = (value - high.astype(F32)).astype(BF16)
            return carry

        lax.fori_loop(first, last, one, 0)

    def greeted():
        pl.semaphore_wait(barrier, count)

    @pl.when(far_relay)
    def _():
        greeted()
        pl.semaphore_signal(ready, inc=1, device_id=(row, relay_from), device_id_type=MESH)

    for copy in small:
        copy.wait()
    put_weights(weights, table, diffusivity)
    rows_step(buf0, buf1, 0, 4, 10, 0)
    rows_step(buf1, buf2, 1, 5, 9, 0)
    rows_step(buf2, low, 2, 6, 8, STEPS)
    @pl.when(jnp.logical_not(far_relay))
    def _():
        greeted()

    to_near = pltpu.make_async_remote_copy(
        src_ref=cov.at[pl.ds(jnp.where(even, strip - STEPS, 0), STEPS)],
        dst_ref=buf0.at[pl.ds(jnp.where(even, 0, strip + STEPS), STEPS)],
        send_sem=row_send.at[0], recv_sem=row_recv.at[0], device_id=near_row, device_id_type=MESH,
    )
    to_next = pltpu.make_async_remote_copy(
        src_ref=edge_out, dst_ref=edge_in,
        send_sem=row_send.at[1], recv_sem=row_recv.at[1], device_id=next_row, device_id_type=MESH,
    )

    @pl.when(has_next)
    def _():
        to_next.start()

    to_near.start()

    def piece(i, side, near):
        lat = chunk_of(i)
        lanes = pl.ds(128 if (side == 0) == near else 0, 128)
        recv = one_recv if near else rest_recv
        return pltpu.make_async_remote_copy(
            src_ref=sb.at[lat, :, lanes], dst_ref=(l2, r2)[side].at[lat, :, lanes],
            send_sem=one_send.at[side], recv_sem=recv.at[side, i],
            device_id=(right, left)[side], device_id_type=MESH,
        )

    def first_message(i, side):
        return piece(i, side, True)

    def to_relay(i, side):
        near, away = ((3, 0), (ncol - 4, ncol - 1))[side]
        return pltpu.make_async_remote_copy(
            src_ref=sb.at[chunk_of(i)], dst_ref=held.at[i // 2],
            send_sem=one_send.at[side], recv_sem=held_recv.at[i // 2],
            device_id=(row, jnp.where(lax.rem(i, 2) == 0, near, away)), device_id_type=MESH,
        )

    def from_relay(j, side, i):
        return pltpu.make_async_remote_copy(
            src_ref=held.at[j], dst_ref=(l2, r2)[side].at[chunk_of(i)],
            send_sem=held_send, recv_sem=one_recv.at[side, i],
            device_id=(row, relay_to), device_id_type=MESH,
        )

    def second_message(i, side):
        lat = chunk_of(i)
        lanes = (pl.ds(128, 128), pl.ds(0, 128))[side]
        return pltpu.make_async_remote_copy(
            src_ref=(l2, r2)[side].at[lat, :, lanes],
            dst_ref=far.at[lat, :, pl.ds(side * 128, 128)],
            send_sem=two_send.at[side], recv_sem=two_recv.at[side, i],
            device_id=(right, left)[side], device_id_type=MESH,
        )

    def send_near(start, stop):
        def one(i, carry):
            @pl.when(next_right)
            def _():
                first_message(i, 0).start()

            @pl.when(next_left)
            def _():
                first_message(i, 1).start()

            return carry

        lax.fori_loop(start, stop, one, 0)

    def send_far(start, stop, by):
        def one(n, carry):
            i = start + n * by

            @pl.when(col == edge)
            def _():
                to_relay(i, 0).start()

            @pl.when(col == edge + 1)
            def _():
                to_relay(i, 1).start()

            return carry

        lax.fori_loop(0, (stop - start + by - 1) // by, one, 0)

    def send_rest(start, stop):
        def one(i, carry):
            @pl.when(next_right)
            def _():
                piece(i, 0, False).start()

            @pl.when(next_left)
            def _():
                piece(i, 1, False).start()

            return carry

        lax.fori_loop(start, stop, one, 0)

    @pl.when(jnp.logical_not(has_up))
    def _():
        buf0[pl.ds(0, STEPS)] = jnp.zeros((STEPS, nlon, width), F32)

    @pl.when(jnp.logical_not(has_down))
    def _():
        buf0[pl.ds(strip + STEPS, STEPS)] = jnp.zeros((STEPS, nlon, width), F32)

    @pl.when(jnp.logical_not(has_left))
    def _():
        l2[...] = jnp.zeros(l2.shape, BF16)

    @pl.when(jnp.logical_not(has_right))
    def _():
        r2[...] = jnp.zeros(r2.shape, BF16)

    @pl.when(col <= 1)
    def _():
        far[:, :, 0:128] = jnp.zeros((strip, nlon, 128), BF16)

    @pl.when(col >= ncol - 2)
    def _():
        far[:, :, 128:256] = jnp.zeros((strip, nlon, 128), BF16)

    send_near(0, 2)
    send_far(0, 1, 1)
    send_rest(0, 2)

    def end_rows(bottom):
        for src, dst, step, top_first, bottom_first, base in (
            (buf0, buf1, 0, 1, strip + 2, 0),
            (buf1, buf2, 1, 2, strip + 1, 0),
            (buf2, low, 2, 3, strip, STEPS),
        ):
            first = jnp.where(bottom, bottom_first, top_first)
            rows_step(src, dst, step, first, first + STEPS, base)

    def pass_to_relay(i, side):
        lanes = (pl.ds(128, 128), pl.ds(0, 128))[side]
        return pltpu.make_async_remote_copy(
            src_ref=(l2, r2)[side].at[chunk_of(i), :, lanes], dst_ref=held_far.at[i],
            send_sem=two_send.at[side], recv_sem=far_recv.at[i],
            device_id=(row, (7, ncol - 8)[side]), device_id_type=MESH,
        )

    def pass_from_relay(i, side):
        return pltpu.make_async_remote_copy(
            src_ref=held_far.at[i], dst_ref=far.at[chunk_of(i), :, pl.ds(side * 128, 128)],
            send_sem=far_send, recv_sem=two_recv.at[side, i],
            device_id=(row, relay_to), device_id_type=MESH,
        )

    def pass_on(i, side, there, onward):
        @pl.when(there)
        def _():
            first_message(i, side).wait_recv()

            @pl.when(onward)
            def _():
                second_message(i, side).start()

            @pl.when(col == edge + side)
            def _():
                pass_to_relay(i, side).start()

    def departure(like, send):
        return pltpu.make_async_remote_copy(
            src_ref=like, dst_ref=like, send_sem=send, recv_sem=far_recv.at[0],
            device_id=right, device_id_type=MESH,
        )

    def dot(x, w):
        return jnp.dot(x, w, preferred_element_type=F32)

    def columns(i):
        lat = chunk_of(i)

        @pl.when(next_left)
        def _():
            piece(i, 0, False).wait_recv()

        @pl.when(next_right)
        def _():
            piece(i, 1, False).wait_recv()

        total = dot(low[lat], w_high[2])
        for place, ref in ((1, l2), (2, sb), (3, r2)):
            x = ref[lat]
            total = total + dot(x, w_high[place]) + dot(x, w_low[place])
        ob[lat] = total
        for half in range(2):

            @pl.when(row * strip + lat == col * 2 + half)
            def _(half=half):
                lanes = pl.ds(half * 128, 128)
                own = lax.broadcasted_iota(jnp.int32, (128, 128), 0) == lax.broadcasted_iota(
                    jnp.int32, (128, 128), 1
                )
                line = noise[pl.ds(lat, 1), :]
                ob[lat, :, lanes] = ob[lat, :, lanes] + jnp.where(own, line, 0.0)

    def far_columns(i):
        lat = chunk_of(i)

        @pl.when(col > 1)
        def _():
            second_message(i, 0).wait_recv()

        @pl.when(col < ncol - 2)
        def _():
            second_message(i, 1).wait_recv()

        x = far[lat]
        ob[lat] = ob[lat] + dot(x, w_high[0]) + dot(x, w_low[0])

    def relay_turn(i):
        for side, here in ((0, lower), (1, jnp.logical_not(lower))):

            @pl.when(here & ((near_relay & (lax.rem(i, 2) == 0)) | (far_relay & (lax.rem(i, 2) == 1))))
            def _(side=side):
                to_relay(i, side).wait_recv()
                from_relay(i // 2, side, i).start()

    def relay_turns(start, stop):
        def one(i, carry):
            relay_turn(i)
            return carry

        lax.fori_loop(start, stop, one, 0)

    relay_turns(0, 1)
    to_near.wait_recv()
    end_rows(even)
    send_near(2, 5)
    send_rest(2, 4)

    @pl.when(at_edge)
    def _():
        pl.semaphore_wait(ready, 1)

    send_far(1, 5, 1)
    relay_turns(1, 3)
    sub = lax.broadcasted_iota(jnp.int32, (8, 128), 0)
    middle = lax.broadcasted_iota(jnp.int32, (8, 128), 1) == 64
    v = [jnp.where((sub == n) & middle, 1.0, 0.0).astype(F32) for n in range(8)]
    for step in range(STEPS):
        fresh = []
        for n in range(1, len(v) - 1):
            mid, east, west, north, south = weights_at(weights, index, step, 2 * col - STEPS + n + step)
            fresh.append(
                mid * v[n]
                + east * pltpu.roll(v[n], 127, 1)
                + west * pltpu.roll(v[n], 1, 1)
                + north * v[n + 1]
                + south * v[n - 1]
            )
        v = fresh
    for place, lat in enumerate((0, 7, 1, 2, 3, 4, 5, 6)):
        for half in range(2):
            line = jnp.broadcast_to(v[half][lat : lat + 1, :], (128, 128))
            block = pltpu.roll(line, 64, 1, stride=1, stride_axis=0)
            rows, lanes = pl.ds((place % 2) * 128, 128), pl.ds(half * 128, 128)
            high = block.astype(BF16)
            w_high[place // 2, rows, lanes] = high
            w_low[place // 2, rows, lanes] = (block - high.astype(F32)).astype(BF16)

    def turn(i, carry):
        @pl.when((i > 1) & (i < 5))
        def _():
            relay_turn(i + 3)

        @pl.when(pass_relay & jnp.logical_not(lower))
        def _():
            def one(n, carry):
                pass_to_relay(n, 1).wait_recv()
                pass_from_relay(n, 1).start()
                return carry

            lax.fori_loop(i + jnp.where(i > 2, 1, 0), jnp.minimum(i + jnp.where(i > 1, 2, 1), strip), one, 0)

        pass_on(i, 0, next_left, next_right)
        pass_on(i, 1, next_right, next_left)
        @pl.when(pass_relay & lower & (i > 0))
        def _():
            pass_to_relay(i - 1, 0).wait_recv()
            pass_from_relay(i - 1, 0).start()

        return carry

    lax.fori_loop(0, 2, turn, 0)

    @pl.when(has_next)
    def _():
        to_next.wait_recv()
        buf0[pl.ds(jnp.where(even, 0, strip + STEPS), STEPS)] = edge_in[...].astype(F32)

    end_rows(jnp.logical_not(even))
    send_near(5, 8)
    send_far(5, 8, 1)
    send_rest(4, 8)
    relay_turns(3, 5)
    lax.fori_loop(2, strip, turn, 0)
    @pl.when(pass_relay & lower)
    def _():
        pass_to_relay(strip - 1, 0).wait_recv()
        pass_from_relay(strip - 1, 0).start()

    def edge_turn(i, carry):
        @pl.when(col == edge + 1)
        def _():
            from_relay(i // 2, 0, i).wait_recv()
            second_message(i, 0).start()

        @pl.when(col == edge)
        def _():
            from_relay(i // 2, 1, i).wait_recv()
            second_message(i, 1).start()

        return carry

    def last_turn(i, carry):
        stop = jnp.where(i < JOINT, i + 1, jnp.where(i == JOINT, strip, i))
        lax.fori_loop(i, stop, edge_turn, 0)

        @pl.when(i < strip)
        def _():
            columns(i)

        @pl.when(i >= LAG)
        def _():
            far_columns(i - LAG)

        return carry

    lax.fori_loop(0, strip + LAG, last_turn, 0)

    for side, there in ((0, has_right), (1, has_left)):

        @pl.when(there)
        def _(side=side):
            departure(sb, one_send.at[side]).wait_send()

        @pl.when(has_left & has_right)
        def _(side=side):
            departure(held_far, two_send.at[side]).wait_send()

    @pl.when(relays)
    def _():
        departure(held, held_send).wait_send()

    @pl.when(pass_relay)
    def _():
        departure(held_far, far_send).wait_send()

    to_near.wait_send()

    @pl.when(has_next)
    def _():
        to_next.wait_send()


def write_out(out_in, s_in, out, s, sem):
    copies = [
        pltpu.make_async_copy(out_in, out, sem.at[0, 0]),
        pltpu.make_async_copy(s_in, s, sem.at[1, 0]),
    ]
    for copy in copies:
        copy.start()
    for copy in copies:
        copy.wait()


def solution(mesh):
    nrow, ncol = mesh.shape["row"], mesh.shape["col"]

    def body(covariance, noise_var, wind_table, diffusivity, wind_index):
        rows_dev, cols_dev = covariance.shape
        strip, nlon = noise_var.shape
        nlat = wind_index.shape[1]
        block = (strip, nlon, cols_dev)
        span = (strip + 2 * STEPS, nlon, cols_dev)
        anywhere = pl.BlockSpec(memory_space=pltpu.HBM)
        held_out, held_s = pl.pallas_call(
            functools.partial(kernel, nlat, nrow, ncol),
            out_shape=(jax.ShapeDtypeStruct(block, F32), jax.ShapeDtypeStruct(block, BF16)),
            in_specs=[anywhere] * 5,
            out_specs=(pl.BlockSpec(memory_space=pltpu.VMEM),) * 2,
            scratch_shapes=[
                pltpu.VMEM(span, F32),
                pltpu.VMEM(span, F32),
                pltpu.VMEM(span, F32),
                pltpu.VMEM(block, BF16),
                pltpu.VMEM(block, BF16),
                pltpu.VMEM(block, BF16),
                pltpu.VMEM(block, BF16),
                pltpu.VMEM((strip // 2, nlon, cols_dev), BF16),
                pltpu.VMEM((strip, nlon, nlon), BF16),
                pltpu.VMEM((STEPS, nlon, cols_dev), BF16),
                pltpu.VMEM((STEPS, nlon, cols_dev), BF16),
                pltpu.VMEM((4, 256, 256), BF16),
                pltpu.VMEM((4, 256, 256), BF16),
                pltpu.VMEM(noise_var.shape, F32),
                pltpu.SMEM(wind_table.shape[::-1], F32),
                pltpu.SMEM(diffusivity.shape, F32),
                pltpu.SMEM(wind_index.shape, jnp.int32),
                pltpu.SMEM((5 * diffusivity.shape[0],), F32),
                pltpu.SemaphoreType.REGULAR,
                pltpu.SemaphoreType.DMA,
                pltpu.SemaphoreType.DMA((4,)),
                pltpu.SemaphoreType.DMA((2,)),
                pltpu.SemaphoreType.DMA((2,)),
                pltpu.SemaphoreType.DMA((2,)),
                pltpu.SemaphoreType.DMA((2, strip)),
                pltpu.SemaphoreType.DMA((2, strip)),
                pltpu.SemaphoreType.DMA((2,)),
                pltpu.SemaphoreType.DMA((2, strip)),
                pltpu.SemaphoreType.DMA,
                pltpu.SemaphoreType.DMA((strip // 2,)),
                pltpu.SemaphoreType.DMA,
                pltpu.SemaphoreType.DMA((strip,)),
            ],
            compiler_params=pltpu.CompilerParams(collective_id=0, has_side_effects=True, vmem_limit_bytes=54755328),
        )(*(
            pltpu.with_memory_space_constraint(x, pltpu.HBM)
            for x in (covariance.reshape(block), noise_var, wind_table.T, diffusivity, wind_index)
        ))
        out, s = pl.pallas_call(
            write_out,
            out_shape=(jax.ShapeDtypeStruct(block, F32), jax.ShapeDtypeStruct(block, BF16)),
            in_specs=[pl.BlockSpec(memory_space=pltpu.VMEM)] * 2,
            out_specs=(anywhere, anywhere),
            scratch_shapes=[pltpu.SemaphoreType.DMA((2, 1))],
            compiler_params=pltpu.CompilerParams(vmem_limit_bytes=1 << 20),
        )(held_out, held_s)
        return out.reshape(rows_dev, cols_dev), s.reshape(rows_dev, cols_dev)

    in_specs = (P("row", "col"), P("row", None), P(), P(), P())
    out_specs = (P("row", "col"), P("row", "col"))
    return jax.shard_map(body, mesh=mesh, in_specs=in_specs, out_specs=out_specs, check_vma=False)
```

```python
import functools

import jax
import jax.numpy as jnp
from jax import lax
from jax.experimental import pallas as pl
from jax.experimental.pallas import tpu as pltpu
from jax.sharding import PartitionSpec as P

MESH = pl.DeviceIdType.MESH
F32 = jnp.float32
BF16 = jnp.bfloat16
STEPS = 3
LAG = 3
JOINT = 5


def chunk_of(i):
    even = lax.rem(lax.axis_index("row"), 2) == 0
    return jnp.where(i < 2, i + 3, jnp.where(even, jnp.where(i < 5, i + 3, i - 5), jnp.where(i < 5, i - 2, i)))


def put_weights(dst, table, diffusivity):
    for regime in range(diffusivity.shape[0]):
        zonal, merid, diffuse = table[0, regime], table[1, regime], diffusivity[regime]
        zz, mm = 0.5 * zonal * zonal, 0.5 * merid * merid
        dst[regime * 5] = 1.0 - zonal * zonal - merid * merid - 4.0 * diffuse
        dst[regime * 5 + 1] = zz - 0.5 * zonal + diffuse
        dst[regime * 5 + 2] = zz + 0.5 * zonal + diffuse
        dst[regime * 5 + 3] = mm - 0.5 * merid + diffuse
        dst[regime * 5 + 4] = mm + 0.5 * merid + diffuse


def weights_at(weights, index, step, lat):
    nlat = index.shape[1]
    inside = jnp.where((lat >= 0) & (lat < nlat), 1.0, 0.0).astype(F32)
    at = index[step, jnp.clip(lat, 0, nlat - 1)] * 5
    return [inside * weights[at + n] for n in range(5)]


def kernel(
    nlat, nrow, ncol,
    cov, noise_in, table_in, diffusivity_in, index_in,
    ob, sb,
    buf0, buf1, buf2, low, l2, r2, far, held, held_far, edge_out, edge_in, w_high, w_low, noise, table, diffusivity, index, weights,
    ready, load_sem, small_sem, row_send, row_recv, one_send, one_recv, rest_recv, two_send, two_recv, held_send, held_recv, far_send, far_recv,
):
    strip, nlon, width = cov.shape
    row, col = lax.axis_index("row"), lax.axis_index("col")
    has_up, has_down = row > 0, row < nrow - 1
    has_left, has_right = col > 0, col < ncol - 1
    next_left, next_right = has_left & (col != ncol // 2), has_right & (col != ncol // 2 - 1)
    even = lax.rem(row, 2) == 0
    has_next = jnp.where(even, row, nrow - 1 - row) > 0
    near_row = (jnp.where(even, row + 1, row - 1), col)
    next_row = (lax.rem(jnp.where(even, row + nrow - 1, row + 1), nrow), col)
    left, right = (row, lax.rem(col + ncol - 1, ncol)), (row, lax.rem(col + 1, ncol))

    edge = ncol // 2 - 1
    near_relay = (col == 3) | (col == ncol - 4)
    far_relay = (col == 0) | (col == ncol - 1)
    pass_relay = (col == 7) | (col == ncol - 8)
    relays = near_relay | far_relay
    at_edge = (col == edge) | (col == edge + 1)
    lower = col <= edge
    relay_from = jnp.where(lower, edge, edge + 1)
    relay_to = jnp.where(lower, edge + 1, edge)

    load = pltpu.make_async_copy(cov, buf0.at[pl.ds(STEPS, strip)], load_sem)
    load.start()
    small = [
        pltpu.make_async_copy(src, dst, small_sem.at[n])
        for n, (src, dst) in enumerate(
            ((index_in, index), (table_in, table), (diffusivity_in, diffusivity), (noise_in, noise))
        )
    ]
    for copy in small:
        copy.start()

    barrier = pltpu.get_barrier_semaphore()

    @pl.when(at_edge)
    def _():
        for peer in (
            jnp.where(lower, ncol - 4, 0),
            jnp.where(lower, ncol - 1, 3),
            jnp.where(lower, ncol - 8, 7),
            jnp.where(lower, 0, ncol - 1),
        ):
            pl.semaphore_signal(barrier, inc=1, device_id=(row, peer), device_id_type=MESH)

    @pl.when(near_relay | pass_relay)
    def _():
        pl.semaphore_signal(barrier, inc=1, device_id=(row, relay_from), device_id_type=MESH)

    count = jnp.where(at_edge | far_relay, 2, 0) + jnp.where(near_relay | pass_relay, 1, 0)
    for there, peer in ((has_next, next_row), (row >= 0, near_row), (next_left, left), (next_right, right)):

        @pl.when(there)
        def _(peer=peer):
            pl.semaphore_signal(barrier, inc=1, device_id=peer, device_id_type=MESH)

        count = count + jnp.where(there, 1, 0)

    def greeted():
        pl.semaphore_wait(barrier, count)

    @pl.when(far_relay)
    def _():
        greeted()
        pl.semaphore_signal(ready, inc=1, device_id=(row, relay_from), device_id_type=MESH)

    load.wait()
    edge_out[...] = buf0[pl.ds(jnp.where(even, STEPS, strip), STEPS)].astype(BF16)
    first_row = row * strip - STEPS

    def rows_step(src, dst, step, first, last, base):
        def one(place, carry):
            mid, east, west, north, south = weights_at(weights, index, step, first_row + place)
            for half in range(width // 128):
                lanes = pl.ds(half * 128, 128)
                value = src[place, :, lanes]
                value = (
                    mid * value
                    + east * pltpu.roll(value, nlon - 1, 0)
                    + west * pltpu.roll(value, 1, 0)
                    + north * src[place + 1, :, lanes]
                    + south * src[place - 1, :, lanes]
                )
                if step < STEPS - 1:
                    dst[place - base, :, lanes] = value
                else:
                    high = value.astype(BF16)
                    sb[place - base, :, lanes] = high
                    dst[place - base, :, lanes] = (value - high.astype(F32)).astype(BF16)
            return carry

        lax.fori_loop(first, last, one, 0)

    for copy in small:
        copy.wait()
    put_weights(weights, table, diffusivity)
    rows_step(buf0, buf1, 0, 4, 10, 0)
    rows_step(buf1, buf2, 1, 5, 9, 0)
    rows_step(buf2, low, 2, 6, 8, STEPS)
    @pl.when(jnp.logical_not(far_relay))
    def _():
        greeted()

    to_near = pltpu.make_async_remote_copy(
        src_ref=cov.at[pl.ds(jnp.where(even, strip - STEPS, 0), STEPS)],
        dst_ref=buf0.at[pl.ds(jnp.where(even, 0, strip + STEPS), STEPS)],
        send_sem=row_send.at[0], recv_sem=row_recv.at[0], device_id=near_row, device_id_type=MESH,
    )
    to_next = pltpu.make_async_remote_copy(
        src_ref=edge_out, dst_ref=edge_in,
        send_sem=row_send.at[1], recv_sem=row_recv.at[1], device_id=next_row, device_id_type=MESH,
    )

    @pl.when(has_next)
    def _():
        to_next.start()

    to_near.start()

    def piece(i, side, near):
        lat = chunk_of(i)
        lanes = pl.ds(128 if (side == 0) == near else 0, 128)
        recv = one_recv if near else rest_recv
        return pltpu.make_async_remote_copy(
            src_ref=sb.at[lat, :, lanes], dst_ref=(l2, r2)[side].at[lat, :, lanes],
            send_sem=one_send.at[side], recv_sem=recv.at[side, i],
            device_id=(right, left)[side], device_id_type=MESH,
        )

    def first_message(i, side):
        return piece(i, side, True)

    def to_relay(i, side):
        near, away = ((3, 0), (ncol - 4, ncol - 1))[side]
        return pltpu.make_async_remote_copy(
            src_ref=sb.at[chunk_of(i)], dst_ref=held.at[i // 2],
            send_sem=one_send.at[side], recv_sem=held_recv.at[i // 2],
            device_id=(row, jnp.where(lax.rem(i, 2) == 0, near, away)), device_id_type=MESH,
        )

    def from_relay(j, side, i):
        return pltpu.make_async_remote_copy(
            src_ref=held.at[j], dst_ref=(l2, r2)[side].at[chunk_of(i)],
            send_sem=held_send, recv_sem=one_recv.at[side, i],
            device_id=(row, relay_to), device_id_type=MESH,
        )

    def second_message(i, side):
        lat = chunk_of(i)
        lanes = (pl.ds(128, 128), pl.ds(0, 128))[side]
        return pltpu.make_async_remote_copy(
            src_ref=(l2, r2)[side].at[lat, :, lanes],
            dst_ref=far.at[lat, :, pl.ds(side * 128, 128)],
            send_sem=two_send.at[side], recv_sem=two_recv.at[side, i],
            device_id=(right, left)[side], device_id_type=MESH,
        )

    def send_near(start, stop):
        def one(i, carry):
            @pl.when(next_right)
            def _():
                first_message(i, 0).start()

            @pl.when(next_left)
            def _():
                first_message(i, 1).start()

            return carry

        lax.fori_loop(start, stop, one, 0)

    def send_far(start, stop, by):
        def one(n, carry):
            i = start + n * by

            @pl.when(col == edge)
            def _():
                to_relay(i, 0).start()

            @pl.when(col == edge + 1)
            def _():
                to_relay(i, 1).start()

            return carry

        lax.fori_loop(0, (stop - start + by - 1) // by, one, 0)

    def send_rest(start, stop):
        def one(i, carry):
            @pl.when(next_right)
            def _():
                piece(i, 0, False).start()

            @pl.when(next_left)
            def _():
                piece(i, 1, False).start()

            return carry

        lax.fori_loop(start, stop, one, 0)

    @pl.when(jnp.logical_not(has_up))
    def _():
        buf0[pl.ds(0, STEPS)] = jnp.zeros((STEPS, nlon, width), F32)

    @pl.when(jnp.logical_not(has_down))
    def _():
        buf0[pl.ds(strip + STEPS, STEPS)] = jnp.zeros((STEPS, nlon, width), F32)

    @pl.when(jnp.logical_not(has_left))
    def _():
        l2[...] = jnp.zeros(l2.shape, BF16)

    @pl.when(jnp.logical_not(has_right))
    def _():
        r2[...] = jnp.zeros(r2.shape, BF16)

    @pl.when(col <= 1)
    def _():
        far[:, :, 0:128] = jnp.zeros((strip, nlon, 128), BF16)

    @pl.when(col >= ncol - 2)
    def _():
        far[:, :, 128:256] = jnp.zeros((strip, nlon, 128), BF16)

    send_near(0, 2)
    send_far(0, 1, 1)
    send_rest(0, 2)

    def end_rows(bottom):
        for src, dst, step, top_first, bottom_first, base in (
            (buf0, buf1, 0, 1, strip + 2, 0),
            (buf1, buf2, 1, 2, strip + 1, 0),
            (buf2, low, 2, 3, strip, STEPS),
        ):
            first = jnp.where(bottom, bottom_first, top_first)
            rows_step(src, dst, step, first, first + STEPS, base)

    def pass_to_relay(i, side):
        lanes = (pl.ds(128, 128), pl.ds(0, 128))[side]
        return pltpu.make_async_remote_copy(
            src_ref=(l2, r2)[side].at[chunk_of(i), :, lanes], dst_ref=held_far.at[i],
            send_sem=two_send.at[side], recv_sem=far_recv.at[i],
            device_id=(row, (7, ncol - 8)[side]), device_id_type=MESH,
        )

    def pass_from_relay(i, side):
        return pltpu.make_async_remote_copy(
            src_ref=held_far.at[i], dst_ref=far.at[chunk_of(i), :, pl.ds(side * 128, 128)],
            send_sem=far_send, recv_sem=two_recv.at[side, i],
            device_id=(row, relay_to), device_id_type=MESH,
        )

    def pass_on(i, side, there, onward):
        @pl.when(there)
        def _():
            first_message(i, side).wait_recv()

            @pl.when(onward)
            def _():
                second_message(i, side).start()

            @pl.when(col == edge + side)
            def _():
                pass_to_relay(i, side).start()

    def departure(like, send):
        return pltpu.make_async_remote_copy(
            src_ref=like, dst_ref=like, send_sem=send, recv_sem=far_recv.at[0],
            device_id=right, device_id_type=MESH,
        )

    def dot(x, w):
        return jnp.dot(x, w, preferred_element_type=F32)

    def columns(i):
        lat = chunk_of(i)

        @pl.when(next_left)
        def _():
            piece(i, 0, False).wait_recv()

        @pl.when(next_right)
        def _():
            piece(i, 1, False).wait_recv()

        total = dot(low[lat], w_high[2])
        for place, ref in ((1, l2), (2, sb), (3, r2)):
            x = ref[lat]
            total = total + dot(x, w_high[place]) + dot(x, w_low[place])
        ob[lat] = total
        for half in range(2):

            @pl.when(row * strip + lat == col * 2 + half)
            def _(half=half):
                lanes = pl.ds(half * 128, 128)
                own = lax.broadcasted_iota(jnp.int32, (128, 128), 0) == lax.broadcasted_iota(
                    jnp.int32, (128, 128), 1
                )
                line = noise[pl.ds(lat, 1), :]
                ob[lat, :, lanes] = ob[lat, :, lanes] + jnp.where(own, line, 0.0)

    def far_columns(i):
        lat = chunk_of(i)

        @pl.when(col > 1)
        def _():
            second_message(i, 0).wait_recv()

        @pl.when(col < ncol - 2)
        def _():
            second_message(i, 1).wait_recv()

        x = far[lat]
        ob[lat] = ob[lat] + dot(x, w_high[0]) + dot(x, w_low[0])

    def relay_turn(i):
        for side, here in ((0, lower), (1, jnp.logical_not(lower))):

            @pl.when(here & ((near_relay & (lax.rem(i, 2) == 0)) | (far_relay & (lax.rem(i, 2) == 1))))
            def _(side=side):
                to_relay(i, side).wait_recv()
                from_relay(i // 2, side, i).start()

    def relay_turns(start, stop):
        def one(i, carry):
            relay_turn(i)
            return carry

        lax.fori_loop(start, stop, one, 0)

    relay_turns(0, 1)
    to_near.wait_recv()
    end_rows(even)
    send_near(2, 5)
    send_rest(2, 4)

    @pl.when(at_edge)
    def _():
        pl.semaphore_wait(ready, 1)

    send_far(1, 5, 1)
    relay_turns(1, 3)
    sub = lax.broadcasted_iota(jnp.int32, (8, 128), 0)
    middle = lax.broadcasted_iota(jnp.int32, (8, 128), 1) == 64
    v = [jnp.where((sub == n) & middle, 1.0, 0.0).astype(F32) for n in range(8)]
    for step in range(STEPS):
        fresh = []
        for n in range(1, len(v) - 1):
            mid, east, west, north, south = weights_at(weights, index, step, 2 * col - STEPS + n + step)
            fresh.append(
                mid * v[n]
                + east * pltpu.roll(v[n], 127, 1)
                + west * pltpu.roll(v[n], 1, 1)
                + north * v[n + 1]
                + south * v[n - 1]
            )
        v = fresh
    for place, lat in enumerate((0, 7, 1, 2, 3, 4, 5, 6)):
        for half in range(2):
            line = jnp.broadcast_to(v[half][lat : lat + 1, :], (128, 128))
            block = pltpu.roll(line, 64, 1, stride=1, stride_axis=0)
            rows, lanes = pl.ds((place % 2) * 128, 128), pl.ds(half * 128, 128)
            high = block.astype(BF16)
            w_high[place // 2, rows, lanes] = high
            w_low[place // 2, rows, lanes] = (block - high.astype(F32)).astype(BF16)

    def turn(i, carry):
        @pl.when((i > 1) & (i < 5))
        def _():
            relay_turn(i + 3)

        @pl.when(pass_relay & jnp.logical_not(lower))
        def _():
            def one(n, carry):
                pass_to_relay(n, 1).wait_recv()
                pass_from_relay(n, 1).start()
                return carry

            lax.fori_loop(i + jnp.where(i > 2, 1, 0), jnp.minimum(i + jnp.where(i > 1, 2, 1), strip), one, 0)

        pass_on(i, 0, next_left, next_right)
        pass_on(i, 1, next_right, next_left)
        @pl.when(pass_relay & lower & (i > 0))
        def _():
            pass_to_relay(i - 1, 0).wait_recv()
            pass_from_relay(i - 1, 0).start()

        return carry

    lax.fori_loop(0, 2, turn, 0)

    @pl.when(has_next)
    def _():
        to_next.wait_recv()
        buf0[pl.ds(jnp.where(even, 0, strip + STEPS), STEPS)] = edge_in[...].astype(F32)

    end_rows(jnp.logical_not(even))
    send_near(5, 8)
    send_far(5, 8, 1)
    send_rest(4, 8)
    relay_turns(3, 5)
    lax.fori_loop(2, strip, turn, 0)
    @pl.when(pass_relay & lower)
    def _():
        pass_to_relay(strip - 1, 0).wait_recv()
        pass_from_relay(strip - 1, 0).start()

    def edge_turn(i, carry):
        @pl.when(col == edge + 1)
        def _():
            from_relay(i // 2, 0, i).wait_recv()
            second_message(i, 0).start()

        @pl.when(col == edge)
        def _():
            from_relay(i // 2, 1, i).wait_recv()
            second_message(i, 1).start()

        return carry

    def last_turn(i, carry):
        stop = jnp.where(i < JOINT, i + 1, jnp.where(i == JOINT, strip, i))
        lax.fori_loop(i, stop, edge_turn, 0)

        @pl.when(i < strip)
        def _():
            columns(i)

        @pl.when(i >= LAG)
        def _():
            far_columns(i - LAG)

        return carry

    lax.fori_loop(0, strip + LAG, last_turn, 0)

    for side, there in ((0, has_right), (1, has_left)):

        @pl.when(there)
        def _(side=side):
            departure(sb, one_send.at[side]).wait_send()

        @pl.when(has_left & has_right)
        def _(side=side):
            departure(held_far, two_send.at[side]).wait_send()

    @pl.when(relays)
    def _():
        departure(held, held_send).wait_send()

    @pl.when(pass_relay)
    def _():
        departure(held_far, far_send).wait_send()

    to_near.wait_send()

    @pl.when(has_next)
    def _():
        to_next.wait_send()


def write_out(out_in, s_in, out, s, sem):
    copies = [
        pltpu.make_async_copy(out_in, out, sem.at[0, 0]),
        pltpu.make_async_copy(s_in, s, sem.at[1, 0]),
    ]
    for copy in copies:
        copy.start()
    for copy in copies:
        copy.wait()


def solution(mesh):
    nrow, ncol = mesh.shape["row"], mesh.shape["col"]

    def body(covariance, noise_var, wind_table, diffusivity, wind_index):
        rows_dev, cols_dev = covariance.shape
        strip, nlon = noise_var.shape
        nlat = wind_index.shape[1]
        block = (strip, nlon, cols_dev)
        span = (strip + 2 * STEPS, nlon, cols_dev)
        anywhere = pl.BlockSpec(memory_space=pltpu.HBM)
        held_out, held_s = pl.pallas_call(
            functools.partial(kernel, nlat, nrow, ncol),
            out_shape=(jax.ShapeDtypeStruct(block, F32), jax.ShapeDtypeStruct(block, BF16)),
            in_specs=[anywhere] * 5,
            out_specs=(pl.BlockSpec(memory_space=pltpu.VMEM),) * 2,
            scratch_shapes=[
                pltpu.VMEM(span, F32),
                pltpu.VMEM(span, F32),
                pltpu.VMEM(span, F32),
                pltpu.VMEM(block, BF16),
                pltpu.VMEM(block, BF16),
                pltpu.VMEM(block, BF16),
                pltpu.VMEM(block, BF16),
                pltpu.VMEM((strip // 2, nlon, cols_dev), BF16),
                pltpu.VMEM((strip, nlon, nlon), BF16),
                pltpu.VMEM((STEPS, nlon, cols_dev), BF16),
                pltpu.VMEM((STEPS, nlon, cols_dev), BF16),
                pltpu.VMEM((4, 256, 256), BF16),
                pltpu.VMEM((4, 256, 256), BF16),
                pltpu.VMEM(noise_var.shape, F32),
                pltpu.SMEM(wind_table.shape[::-1], F32),
                pltpu.SMEM(diffusivity.shape, F32),
                pltpu.SMEM(wind_index.shape, jnp.int32),
                pltpu.SMEM((5 * diffusivity.shape[0],), F32),
                pltpu.SemaphoreType.REGULAR,
                pltpu.SemaphoreType.DMA,
                pltpu.SemaphoreType.DMA((4,)),
                pltpu.SemaphoreType.DMA((2,)),
                pltpu.SemaphoreType.DMA((2,)),
                pltpu.SemaphoreType.DMA((2,)),
                pltpu.SemaphoreType.DMA((2, strip)),
                pltpu.SemaphoreType.DMA((2, strip)),
                pltpu.SemaphoreType.DMA((2,)),
                pltpu.SemaphoreType.DMA((2, strip)),
                pltpu.SemaphoreType.DMA,
                pltpu.SemaphoreType.DMA((strip // 2,)),
                pltpu.SemaphoreType.DMA,
                pltpu.SemaphoreType.DMA((strip,)),
            ],
            compiler_params=pltpu.CompilerParams(collective_id=0, has_side_effects=True, vmem_limit_bytes=54755328),
        )(*(
            pltpu.with_memory_space_constraint(x, pltpu.HBM)
            for x in (covariance.reshape(block), noise_var, wind_table.T, diffusivity, wind_index)
        ))
        out, s = pl.pallas_call(
            write_out,
            out_shape=(jax.ShapeDtypeStruct(block, F32), jax.ShapeDtypeStruct(block, BF16)),
            in_specs=[pl.BlockSpec(memory_space=pltpu.VMEM)] * 2,
            out_specs=(anywhere, anywhere),
            scratch_shapes=[pltpu.SemaphoreType.DMA((2, 1))],
            compiler_params=pltpu.CompilerParams(vmem_limit_bytes=1 << 20),
        )(held_out, held_s)
        return out.reshape(rows_dev, cols_dev), s.reshape(rows_dev, cols_dev)

    in_specs = (P("row", "col"), P("row", None), P(), P(), P())
    out_specs = (P("row", "col"), P("row", "col"))
    return jax.shard_map(body, mesh=mesh, in_specs=in_specs, out_specs=out_specs, check_vma=False)
```

```python
import functools

import jax
import jax.numpy as jnp
from jax import lax
from jax.experimental import pallas as pl
from jax.experimental.pallas import tpu as pltpu
from jax.sharding import PartitionSpec as P

MESH = pl.DeviceIdType.MESH
F32 = jnp.float32
BF16 = jnp.bfloat16
STEPS = 3
LAG = 3
JOINT = 3


def chunk_of(i):
    even = lax.rem(lax.axis_index("row"), 2) == 0
    return jnp.where(i < 2, i + 3, jnp.where(even, jnp.where(i < 5, i + 3, i - 5), jnp.where(i < 5, i - 2, i)))


def put_weights(dst, table, diffusivity):
    for regime in range(diffusivity.shape[0]):
        zonal, merid, diffuse = table[0, regime], table[1, regime], diffusivity[regime]
        zz, mm = 0.5 * zonal * zonal, 0.5 * merid * merid
        dst[regime * 5] = 1.0 - zonal * zonal - merid * merid - 4.0 * diffuse
        dst[regime * 5 + 1] = zz - 0.5 * zonal + diffuse
        dst[regime * 5 + 2] = zz + 0.5 * zonal + diffuse
        dst[regime * 5 + 3] = mm - 0.5 * merid + diffuse
        dst[regime * 5 + 4] = mm + 0.5 * merid + diffuse


def weights_at(weights, index, step, lat):
    nlat = index.shape[1]
    inside = jnp.where((lat >= 0) & (lat < nlat), 1.0, 0.0).astype(F32)
    at = index[step, jnp.clip(lat, 0, nlat - 1)] * 5
    return [inside * weights[at + n] for n in range(5)]


def kernel(
    nlat, nrow, ncol,
    cov, noise_in, table_in, diffusivity_in, index_in,
    ob, sb,
    buf0, buf1, buf2, low, l2, r2, far, held, held_far, edge_out, edge_in, w_high, w_low, noise, table, diffusivity, index, weights,
    ready, load_sem, small_sem, row_send, row_recv, one_send, one_recv, rest_recv, two_send, two_recv, held_send, far_send, far_recv,
):
    strip, nlon, width = cov.shape
    row, col = lax.axis_index("row"), lax.axis_index("col")
    has_up, has_down = row > 0, row < nrow - 1
    has_left, has_right = col > 0, col < ncol - 1
    next_left, next_right = has_left & (col != ncol // 2), has_right & (col != ncol // 2 - 1)
    even = lax.rem(row, 2) == 0
    has_next = jnp.where(even, row, nrow - 1 - row) > 0
    near_row = (jnp.where(even, row + 1, row - 1), col)
    next_row = (lax.rem(jnp.where(even, row + nrow - 1, row + 1), nrow), col)
    left, right = (row, lax.rem(col + ncol - 1, ncol)), (row, lax.rem(col + 1, ncol))

    edge = ncol // 2 - 1
    near_relay = (col == 3) | (col == ncol - 4)
    far_relay = (col == 0) | (col == ncol - 1)
    pass_relay = (col == 7) | (col == ncol - 8)
    relays = near_relay | far_relay
    at_edge = (col == edge) | (col == edge + 1)
    lower = col <= edge
    relay_from = jnp.where(lower, edge, edge + 1)
    relay_to = jnp.where(lower, edge + 1, edge)

    load = pltpu.make_async_copy(cov, buf0.at[pl.ds(STEPS, strip)], load_sem)
    load.start()
    small = [
        pltpu.make_async_copy(src, dst, small_sem.at[n])
        for n, (src, dst) in enumerate(
            ((index_in, index), (table_in, table), (diffusivity_in, diffusivity), (noise_in, noise))
        )
    ]
    for copy in small:
        copy.start()

    barrier = pltpu.get_barrier_semaphore()

    @pl.when(at_edge)
    def _():
        for peer in (
            jnp.where(lower, ncol - 4, 0),
            jnp.where(lower, ncol - 1, 3),
            jnp.where(lower, ncol - 8, 7),
            jnp.where(lower, 0, ncol - 1),
        ):
            pl.semaphore_signal(barrier, inc=1, device_id=(row, peer), device_id_type=MESH)

    @pl.when(near_relay | pass_relay)
    def _():
        pl.semaphore_signal(barrier, inc=1, device_id=(row, relay_from), device_id_type=MESH)

    count = jnp.where(at_edge | far_relay, 2, 0) + jnp.where(near_relay | pass_relay, 1, 0)
    for there, peer in ((has_next, next_row), (row >= 0, near_row), (next_left, left), (next_right, right)):

        @pl.when(there)
        def _(peer=peer):
            pl.semaphore_signal(barrier, inc=1, device_id=peer, device_id_type=MESH)

        count = count + jnp.where(there, 1, 0)

    def greeted():
        pl.semaphore_wait(barrier, count)

    @pl.when(far_relay)
    def _():
        greeted()
        pl.semaphore_signal(ready, inc=1, device_id=(row, relay_from), device_id_type=MESH)

    load.wait()
    edge_out[...] = buf0[pl.ds(jnp.where(even, STEPS, strip), STEPS)].astype(BF16)
    first_row = row * strip - STEPS

    def rows_step(src, dst, step, first, last, base):
        def one(place, carry):
            mid, east, west, north, south = weights_at(weights, index, step, first_row + place)
            for half in range(width // 128):
                lanes = pl.ds(half * 128, 128)
                value = src[place, :, lanes]
                value = (
                    mid * value
                    + east * pltpu.roll(value, nlon - 1, 0)
                    + west * pltpu.roll(value, 1, 0)
                    + north * src[place + 1, :, lanes]
                    + south * src[place - 1, :, lanes]
                )
                if step < STEPS - 1:
                    dst[place - base, :, lanes] = value
                else:
                    high = value.astype(BF16)
                    sb[place - base, :, lanes] = high
                    dst[place - base, :, lanes] = (value - high.astype(F32)).astype(BF16)
            return carry

        lax.fori_loop(first, last, one, 0)

    for copy in small:
        copy.wait()
    put_weights(weights, table, diffusivity)
    rows_step(buf0, buf1, 0, 4, 10, 0)
    rows_step(buf1, buf2, 1, 5, 9, 0)
    rows_step(buf2, low, 2, 6, 8, STEPS)
    @pl.when(jnp.logical_not(far_relay))
    def _():
        greeted()

    to_near = pltpu.make_async_remote_copy(
        src_ref=cov.at[pl.ds(jnp.where(even, strip - STEPS, 0), STEPS)],
        dst_ref=buf0.at[pl.ds(jnp.where(even, 0, strip + STEPS), STEPS)],
        send_sem=row_send.at[0], recv_sem=row_recv.at[0], device_id=near_row, device_id_type=MESH,
    )
    to_next = pltpu.make_async_remote_copy(
        src_ref=edge_out, dst_ref=edge_in,
        send_sem=row_send.at[1], recv_sem=row_recv.at[1], device_id=next_row, device_id_type=MESH,
    )

    @pl.when(has_next)
    def _():
        to_next.start()

    to_near.start()

    def piece(i, side, near):
        lat = chunk_of(i)
        lanes = pl.ds(128 if (side == 0) == near else 0, 128)
        recv = one_recv if near else rest_recv
        return pltpu.make_async_remote_copy(
            src_ref=sb.at[lat, :, lanes], dst_ref=(l2, r2)[side].at[lat, :, lanes],
            send_sem=one_send.at[side], recv_sem=recv.at[side, i],
            device_id=(right, left)[side], device_id_type=MESH,
        )

    def first_message(i, side):
        return piece(i, side, True)

    def to_relay(i, side):
        near, away = ((3, 0), (ncol - 4, ncol - 1))[side]
        return pltpu.make_async_remote_copy(
            src_ref=sb.at[chunk_of(i)], dst_ref=held.at[i // 2],
            send_sem=one_send.at[side], recv_sem=far_recv.at[i // 2],
            device_id=(row, jnp.where(lax.rem(i, 2) == 0, near, away)), device_id_type=MESH,
        )

    def from_relay(j, side, i):
        return pltpu.make_async_remote_copy(
            src_ref=held.at[j], dst_ref=(l2, r2)[side].at[chunk_of(i)],
            send_sem=held_send, recv_sem=one_recv.at[side, i],
            device_id=(row, relay_to), device_id_type=MESH,
        )

    def second_message(i, side):
        lat = chunk_of(i)
        lanes = (pl.ds(128, 128), pl.ds(0, 128))[side]
        return pltpu.make_async_remote_copy(
            src_ref=(l2, r2)[side].at[lat, :, lanes],
            dst_ref=far.at[lat, :, pl.ds(side * 128, 128)],
            send_sem=two_send.at[side], recv_sem=two_recv.at[side, i],
            device_id=(right, left)[side], device_id_type=MESH,
        )

    def send_near(start, stop):
        def one(i, carry):
            @pl.when(next_right)
            def _():
                first_message(i, 0).start()

            @pl.when(next_left)
            def _():
                first_message(i, 1).start()

            return carry

        lax.fori_loop(start, stop, one, 0)

    def send_far(start, stop, by):
        def one(n, carry):
            i = start + n * by

            @pl.when(col == edge)
            def _():
                to_relay(i, 0).start()

            @pl.when(col == edge + 1)
            def _():
                to_relay(i, 1).start()

            return carry

        lax.fori_loop(0, (stop - start + by - 1) // by, one, 0)

    def send_rest(start, stop):
        def one(i, carry):
            @pl.when(next_right)
            def _():
                piece(i, 0, False).start()

            @pl.when(next_left)
            def _():
                piece(i, 1, False).start()

            return carry

        lax.fori_loop(start, stop, one, 0)

    @pl.when(jnp.logical_not(has_up))
    def _():
        buf0[pl.ds(0, STEPS)] = jnp.zeros((STEPS, nlon, width), F32)

    @pl.when(jnp.logical_not(has_down))
    def _():
        buf0[pl.ds(strip + STEPS, STEPS)] = jnp.zeros((STEPS, nlon, width), F32)

    @pl.when(jnp.logical_not(has_left))
    def _():
        l2[...] = jnp.zeros(l2.shape, BF16)

    @pl.when(jnp.logical_not(has_right))
    def _():
        r2[...] = jnp.zeros(r2.shape, BF16)

    @pl.when(col <= 1)
    def _():
        far[:, :, 0:128] = jnp.zeros((strip, nlon, 128), BF16)

    @pl.when(col >= ncol - 2)
    def _():
        far[:, :, 128:256] = jnp.zeros((strip, nlon, 128), BF16)

    send_near(0, 2)
    send_far(0, 1, 1)
    send_rest(0, 2)

    def end_rows(bottom):
        for src, dst, step, top_first, bottom_first, base in (
            (buf0, buf1, 0, 1, strip + 2, 0),
            (buf1, buf2, 1, 2, strip + 1, 0),
            (buf2, low, 2, 3, strip, STEPS),
        ):
            first = jnp.where(bottom, bottom_first, top_first)
            rows_step(src, dst, step, first, first + STEPS, base)

    def pass_to_relay(i, side):
        lanes = (pl.ds(128, 128), pl.ds(0, 128))[side]
        return pltpu.make_async_remote_copy(
            src_ref=(l2, r2)[side].at[chunk_of(i), :, lanes], dst_ref=held_far.at[i],
            send_sem=two_send.at[side], recv_sem=far_recv.at[i],
            device_id=(row, (7, ncol - 8)[side]), device_id_type=MESH,
        )

    def pass_from_relay(i, side):
        return pltpu.make_async_remote_copy(
            src_ref=held_far.at[i], dst_ref=far.at[chunk_of(i), :, pl.ds(side * 128, 128)],
            send_sem=far_send, recv_sem=two_recv.at[side, i],
            device_id=(row, relay_to), device_id_type=MESH,
        )

    def pass_on(i, side, there, onward):
        @pl.when(there)
        def _():
            first_message(i, side).wait_recv()

            @pl.when(onward)
            def _():
                second_message(i, side).start()

            @pl.when(col == edge + side)
            def _():
                pass_to_relay(i, side).start()

    def departure(like, send):
        return pltpu.make_async_remote_copy(
            src_ref=like, dst_ref=like, send_sem=send, recv_sem=far_recv.at[0],
            device_id=right, device_id_type=MESH,
        )

    def dot(x, w):
        return jnp.dot(x, w, preferred_element_type=F32)

    def columns(i):
        lat = chunk_of(i)

        @pl.when(next_left)
        def _():
            piece(i, 0, False).wait_recv()

        @pl.when(next_right)
        def _():
            piece(i, 1, False).wait_recv()

        total = dot(low[lat], w_high[2])
        for place, ref in ((1, l2), (2, sb), (3, r2)):
            x = ref[lat]
            total = total + dot(x, w_high[place]) + dot(x, w_low[place])
        ob[lat] = total
        for half in range(2):

            @pl.when(row * strip + lat == col * 2 + half)
            def _(half=half):
                lanes = pl.ds(half * 128, 128)
                own = lax.broadcasted_iota(jnp.int32, (128, 128), 0) == lax.broadcasted_iota(
                    jnp.int32, (128, 128), 1
                )
                line = noise[pl.ds(lat, 1), :]
                ob[lat, :, lanes] = ob[lat, :, lanes] + jnp.where(own, line, 0.0)

    def far_columns(i):
        lat = chunk_of(i)

        @pl.when(col > 1)
        def _():
            second_message(i, 0).wait_recv()

        @pl.when(col < ncol - 2)
        def _():
            second_message(i, 1).wait_recv()

        x = far[lat]
        ob[lat] = ob[lat] + dot(x, w_high[0]) + dot(x, w_low[0])

    def relay_turn(i):
        for side, here in ((0, lower), (1, jnp.logical_not(lower))):

            @pl.when(here & ((near_relay & (lax.rem(i, 2) == 0)) | (far_relay & (lax.rem(i, 2) == 1))))
            def _(side=side):
                to_relay(i, side).wait_recv()
                from_relay(i // 2, side, i).start()

    def relay_turns(start, stop):
        def one(i, carry):
            relay_turn(i)
            return carry

        lax.fori_loop(start, stop, one, 0)

    relay_turns(0, 1)
    to_near.wait_recv()
    end_rows(even)
    send_near(2, 5)
    send_rest(2, 4)

    @pl.when(at_edge)
    def _():
        pl.semaphore_wait(ready, 1)

    send_far(1, 5, 1)
    relay_turns(1, 3)
    sub = lax.broadcasted_iota(jnp.int32, (8, 128), 0)
    middle = lax.broadcasted_iota(jnp.int32, (8, 128), 1) == 64
    v = [jnp.where((sub == n) & middle, 1.0, 0.0).astype(F32) for n in range(8)]
    for step in range(STEPS):
        fresh = []
        for n in range(1, len(v) - 1):
            mid, east, west, north, south = weights_at(weights, index, step, 2 * col - STEPS + n + step)
            fresh.append(
                mid * v[n]
                + east * pltpu.roll(v[n], 127, 1)
                + west * pltpu.roll(v[n], 1, 1)
                + north * v[n + 1]
                + south * v[n - 1]
            )
        v = fresh
    for place, lat in enumerate((0, 7, 1, 2, 3, 4, 5, 6)):
        for half in range(2):
            line = jnp.broadcast_to(v[half][lat : lat + 1, :], (128, 128))
            block = pltpu.roll(line, 64, 1, stride=1, stride_axis=0)
            rows, lanes = pl.ds((place % 2) * 128, 128), pl.ds(half * 128, 128)
            high = block.astype(BF16)
            w_high[place // 2, rows, lanes] = high
            w_low[place // 2, rows, lanes] = (block - high.astype(F32)).astype(BF16)

    def turn(i, carry):
        @pl.when((i > 1) & (i < 5))
        def _():
            relay_turn(i + 3)

        @pl.when(pass_relay & jnp.logical_not(lower))
        def _():
            def one(n, carry):
                pass_to_relay(n, 1).wait_recv()
                pass_from_relay(n, 1).start()
                return carry

            lax.fori_loop(i + jnp.where(i > 2, 1, 0), jnp.minimum(i + jnp.where(i > 1, 2, 1), strip), one, 0)

        pass_on(i, 0, next_left, next_right)
        pass_on(i, 1, next_right, next_left)
        @pl.when(pass_relay & lower & (i > 0))
        def _():
            pass_to_relay(i - 1, 0).wait_recv()
            pass_from_relay(i - 1, 0).start()

        return carry

    lax.fori_loop(0, 2, turn, 0)

    @pl.when(has_next)
    def _():
        to_next.wait_recv()
        buf0[pl.ds(jnp.where(even, 0, strip + STEPS), STEPS)] = edge_in[...].astype(F32)

    end_rows(jnp.logical_not(even))
    send_near(5, 8)
    send_far(5, 8, 1)
    send_rest(4, 8)
    relay_turns(3, 5)
    lax.fori_loop(2, strip, turn, 0)
    @pl.when(pass_relay & lower)
    def _():
        pass_to_relay(strip - 1, 0).wait_recv()
        pass_from_relay(strip - 1, 0).start()

    def edge_turn(i, carry):
        @pl.when(col == edge + 1)
        def _():
            from_relay(i // 2, 0, i).wait_recv()
            second_message(i, 0).start()

        @pl.when(col == edge)
        def _():
            from_relay(i // 2, 1, i).wait_recv()
            second_message(i, 1).start()

        return carry

    def last_turn(i, carry):
        stop = jnp.where(i < JOINT, i + 1, jnp.where(i == JOINT, strip, i))
        lax.fori_loop(i, stop, edge_turn, 0)

        @pl.when(i < strip)
        def _():
            columns(i)

        @pl.when(i >= LAG)
        def _():
            far_columns(i - LAG)

        return carry

    lax.fori_loop(0, strip + LAG, last_turn, 0)

    for side, there in ((0, has_right), (1, has_left)):

        @pl.when(there)
        def _(side=side):
            departure(sb, one_send.at[side]).wait_send()

        @pl.when(has_left & has_right)
        def _(side=side):
            departure(held_far, two_send.at[side]).wait_send()

    @pl.when(relays)
    def _():
        departure(held, held_send).wait_send()

    @pl.when(pass_relay)
    def _():
        departure(held_far, far_send).wait_send()

    to_near.wait_send()

    @pl.when(has_next)
    def _():
        to_next.wait_send()


def write_out(out_in, s_in, out, s, sem):
    copies = [
        pltpu.make_async_copy(out_in, out, sem.at[0, 0]),
        pltpu.make_async_copy(s_in, s, sem.at[1, 0]),
    ]
    for copy in copies:
        copy.start()
    for copy in copies:
        copy.wait()


def solution(mesh):
    nrow, ncol = mesh.shape["row"], mesh.shape["col"]

    def body(covariance, noise_var, wind_table, diffusivity, wind_index):
        rows_dev, cols_dev = covariance.shape
        strip, nlon = noise_var.shape
        nlat = wind_index.shape[1]
        block = (strip, nlon, cols_dev)
        span = (strip + 2 * STEPS, nlon, cols_dev)
        anywhere = pl.BlockSpec(memory_space=pltpu.HBM)
        held_out, held_s = pl.pallas_call(
            functools.partial(kernel, nlat, nrow, ncol),
            out_shape=(jax.ShapeDtypeStruct(block, F32), jax.ShapeDtypeStruct(block, BF16)),
            in_specs=[anywhere] * 5,
            out_specs=(pl.BlockSpec(memory_space=pltpu.VMEM),) * 2,
            scratch_shapes=[
                pltpu.VMEM(span, F32),
                pltpu.VMEM(span, F32),
                pltpu.VMEM(span, F32),
                pltpu.VMEM(block, BF16),
                pltpu.VMEM(block, BF16),
                pltpu.VMEM(block, BF16),
                pltpu.VMEM(block, BF16),
                pltpu.VMEM((strip // 2, nlon, cols_dev), BF16),
                pltpu.VMEM((strip, nlon, nlon), BF16),
                pltpu.VMEM((STEPS, nlon, cols_dev), BF16),
                pltpu.VMEM((STEPS, nlon, cols_dev), BF16),
                pltpu.VMEM((4, 256, 256), BF16),
                pltpu.VMEM((4, 256, 256), BF16),
                pltpu.VMEM(noise_var.shape, F32),
                pltpu.SMEM(wind_table.shape[::-1], F32),
                pltpu.SMEM(diffusivity.shape, F32),
                pltpu.SMEM(wind_index.shape, jnp.int32),
                pltpu.SMEM((5 * diffusivity.shape[0],), F32),
                pltpu.SemaphoreType.REGULAR,
                pltpu.SemaphoreType.DMA,
                pltpu.SemaphoreType.DMA((4,)),
                pltpu.SemaphoreType.DMA((2,)),
                pltpu.SemaphoreType.DMA((2,)),
                pltpu.SemaphoreType.DMA((2,)),
                pltpu.SemaphoreType.DMA((2, strip)),
                pltpu.SemaphoreType.DMA((2, strip)),
                pltpu.SemaphoreType.DMA((2,)),
                pltpu.SemaphoreType.DMA((2, strip)),
                pltpu.SemaphoreType.DMA,
                pltpu.SemaphoreType.DMA,
                pltpu.SemaphoreType.DMA((strip,)),
            ],
            compiler_params=pltpu.CompilerParams(collective_id=0, has_side_effects=True, vmem_limit_bytes=54755328),
        )(*(
            pltpu.with_memory_space_constraint(x, pltpu.HBM)
            for x in (covariance.reshape(block), noise_var, wind_table.T, diffusivity, wind_index)
        ))
        out, s = pl.pallas_call(
            write_out,
            out_shape=(jax.ShapeDtypeStruct(block, F32), jax.ShapeDtypeStruct(block, BF16)),
            in_specs=[pl.BlockSpec(memory_space=pltpu.VMEM)] * 2,
            out_specs=(anywhere, anywhere),
            scratch_shapes=[pltpu.SemaphoreType.DMA((2, 1))],
            compiler_params=pltpu.CompilerParams(vmem_limit_bytes=1 << 20),
        )(held_out, held_s)
        return out.reshape(rows_dev, cols_dev), s.reshape(rows_dev, cols_dev)

    in_specs = (P("row", "col"), P("row", None), P(), P(), P())
    out_specs = (P("row", "col"), P("row", "col"))
    return jax.shard_map(body, mesh=mesh, in_specs=in_specs, out_specs=out_specs, check_vma=False)
```
